32 devices in a mesh: group: 4 (over z), replica: 8 (over y, x, core).
Axes of the slice: x: 2, y: 2, z: 4, core: 2. Of those that a mesh axis runs over, the one named last changes fastest.
Arguments:
- layer_input: bfloat16 [8, 1024, 2560], P('replica', 'group')
- positions: int32 [8, 1024], P('replica', 'group'), may hold values from 0 to 543, as said below
- piece_starts: int32 [8, 2], P('replica'), may hold values from 0 to 768, as said below
- gain_attn: bfloat16 [2560], P('group'), may hold values from 0.5 to 1.5
- w_query: bfloat16 [2560, 2560], P('group'), may hold values from -0.125 to 0.125
- w_key: bfloat16 [2560, 640], P('group'), may hold values from -0.125 to 0.125
- w_value: bfloat16 [2560, 640], P('group'), may hold values from -0.125 to 0.125
- w_out: bfloat16 [2560, 2560], P('group'), may hold values from -2 to 2
- gain_mlp: bfloat16 [2560], P('group'), may hold values from 0.5 to 1.5
- w_gate: bfloat16 [2560, 7168], P('group'), may hold values from -0.125 to 0.125
- w_up: bfloat16 [2560, 7168], P('group'), may hold values from -0.125 to 0.125
- w_down: bfloat16 [2560, 7168], P('group'), may hold values from -0.0625 to 0.0625
- out_grad: bfloat16 [8, 1024, 2560], P('replica', 'group'), may hold values from -6 to 6
Outputs:
- layer_out: bfloat16 [8, 1024, 2560], P('replica', 'group')
- input_grad: float32 [8, 1024, 2560], P('replica', 'group')
- grad_norm_attn: float32 [2560], P(('group', 'replica'))
- grad_query: float32 [2560, 2560], P(('group', 'replica'))
- grad_key: float32 [2560, 640], P(('group', 'replica'))
- grad_value: float32 [2560, 640], P(('group', 'replica'))
- grad_out: float32 [2560, 2560], P(('group', 'replica'))
- grad_norm_mlp: float32 [2560], P(('group', 'replica'))
- grad_gate: float32 [2560, 7168], P(('group', 'replica'))
- grad_up: float32 [2560, 7168], P(('group', 'replica'))
- grad_down: float32 [2560, 7168], P(('group', 'replica'))
- stream_rms: float32 [8, 3], P('replica')
The draws below stay inside these ranges and needn't reach their ends.
Inputs may be any that keep to these rules, and one draw needn't show every extreme that they name: `piece_starts`: each sequence holds two picture pieces of 256 tokens that start at multiples of 128, the second starting 256 or more tokens after the first, both ending inside the sequence. `positions`: outside picture pieces a token's position is one more than the previous token's; the j-th token of a piece whose first token has position p gets p + j // 16, and the token after the piece gets p + 16; a sequence's first token has position 0.
All inputs are finite; a program needn't handle non-finite values.
Results may differ from the reference program's by a relative error of at most 0.018.
Values may be sent and summed in bfloat16 or wider, within the bound.
No kernel may reach another device: no remote copies, remote signals or barrier semaphores. Data moves between devices by JAX's collectives and lax.ppermute only.
A program may use at most 384 MiB of HBM per device.

```python
import jax
import jax.numpy as jnp
from jax import lax

D = 2560
HEADS = 32
KV_HEADS = 8
HEAD_DIM = 80
FF = 7168
LEN = 1024
SLOT = 128
PIECE_ROWS = 16
PIECE = 256
BATCH = 8


def piece_layout(key):
    slot_count = LEN // SLOT
    span = PIECE // SLOT
    first = jax.random.randint(jax.random.fold_in(key, 11), (BATCH,), 0, slot_count - 2 * span + 1)
    extra = jax.random.randint(jax.random.fold_in(key, 12), (BATCH,), 0, slot_count - 2 * span + 1 - first)
    second = first + span + extra
    return (jnp.stack([first, second], axis=1) * SLOT).astype(jnp.int32)


def draw_piece_starts(key, part):
    return piece_layout(key)


def draw_positions(key, part):
    starts = piece_layout(key)
    tokens_at = jnp.arange(LEN, dtype=jnp.int32)[None, :]
    first = starts[:, :1]
    second = starts[:, 1:]
    saved = PIECE - PIECE_ROWS
    placed = tokens_at + 0 * first
    placed = jnp.where(tokens_at >= first, first + (tokens_at - first) // PIECE_ROWS, placed)
    placed = jnp.where(tokens_at >= first + PIECE, tokens_at - saved, placed)
    placed = jnp.where(tokens_at >= second, second - saved + (tokens_at - second) // PIECE_ROWS, placed)
    placed = jnp.where(tokens_at >= second + PIECE, tokens_at - 2 * saved, placed)
    return placed.astype(jnp.int32)


def draw_layer_input(key, part):
    noise_key = jax.random.fold_in(key, 21)
    row_key = jax.random.fold_in(key, 22)
    along = jnp.arange(LEN, dtype=jnp.float32) / LEN
    base = jax.random.normal(noise_key, (BATCH, LEN, D), jnp.float32)
    rising = 0.7 * 3.0 ** along
    row_scale = jnp.exp(jax.random.uniform(row_key, (BATCH, LEN, 1), jnp.float32, -0.35, 0.35))
    return (base * rising[None, :, None] * row_scale).astype(jnp.bfloat16)


def block_scale(key, shape, pieces, low, top_value):
    loudness = 1.0
    for dim, shards_of in pieces:
        heights = jax.random.uniform(jax.random.fold_in(jax.random.fold_in(key, 6), dim), (shards_of,), jnp.float32, low / len(pieces), top_value / len(pieces))
        loudness = loudness * jnp.repeat(jnp.exp(heights), shape[dim] // shards_of).reshape((-1,) + (1,) * (len(shape) - 1 - dim))
    return loudness


def gaussian(stream_key, dims, scale, bound, pieces=(), kind=jnp.bfloat16):
    values = jax.random.normal(stream_key, dims, jnp.float32) * scale
    if len(pieces) > 0:
        values = block_scale(stream_key, dims, pieces, -0.22, 0.18) * values
    return jnp.clip(values, min=-bound, max=bound).astype(kind)


def setup_inputs(seed: int = 0) -> dict:
    seeds = jax.random.split(jax.random.key(seed), 14)
    return {
        "layer_input": draw_layer_input(jax.random.fold_in(seeds[13], 71), 0),
        "positions": draw_positions(jax.random.fold_in(seeds[13], 71), 0),
        "piece_starts": draw_piece_starts(jax.random.fold_in(seeds[13], 71), 0),
        "gain_attn": jnp.clip(1.0 + 0.1 * jax.random.normal(seeds[3], (D,), jnp.float32), 0.5, 1.5).astype(jnp.bfloat16),
        "w_query": gaussian(seeds[4], (D, D), D ** -0.5, 0.125, ((0, 4),)),
        "w_key": gaussian(seeds[5], (D, KV_HEADS * HEAD_DIM), D ** -0.5, 0.125, ((0, 4),)),
        "w_value": gaussian(seeds[6], (D, KV_HEADS * HEAD_DIM), D ** -0.5, 0.125, ((0, 4),)),
        "w_out": gaussian(seeds[7], (D, D), (max(D // 256, 1)) ** -0.5, 2.0, ((0, 4),)),
        "gain_mlp": jnp.clip(1.0 + 0.1 * jax.random.normal(seeds[8], (D,), jnp.float32), 0.5, 1.5).astype(jnp.bfloat16),
        "w_gate": gaussian(seeds[9], (D, FF), D ** -0.5, 0.125, ((0, 4),)),
        "w_up": gaussian(seeds[10], (D, FF), D ** -0.5, 0.125, ((0, 4),)),
        "w_down": gaussian(seeds[11], (D, FF), FF ** -0.5, 0.0625, ((0, 4),)),
        "out_grad": gaussian(seeds[12], (BATCH, LEN, D), 1.0, 6.0, ((0, 8), (1, 4))),
    }


@jax.custom_vjp
def low(v):
    return lax.optimization_barrier(v.astype(jnp.bfloat16)).astype(jnp.float32)

@jax.custom_vjp
def low_back(v):
    return v

def low_keep(v):
    return (low(v), None)

def low_pass(kept, grad):
    return (grad,)

def back_keep(v):
    return (v, None)

def back_low(kept, grad):
    return (low(grad),)
low.defvjp(low_keep, low_pass)
low_back.defvjp(back_keep, back_low)
epsilon = 1e-05
rope_base = 1000000.0
highest = lax.Precision.HIGHEST

def product(left, right):
    return jnp.dot(left, right, precision=highest)

def inverse_rms(values):
    return lax.rsqrt(lax.optimization_barrier(jnp.mean(values * values, axis=-1, keepdims=True)) + epsilon)

def rope_tables(places):
    halves = HEAD_DIM // 2
    frequency = rope_base ** (-(jnp.arange(halves, dtype=jnp.float32) * 2.0 / HEAD_DIM))
    angles = places.astype(jnp.float32)[:, None] * frequency[None, :]
    angles = jnp.concatenate([angles, angles], axis=-1)
    return (jnp.cos(angles), jnp.sin(angles))

def rotate(values, cosine, sine):
    halves = HEAD_DIM // 2
    turned = jnp.concatenate([-values[..., halves:], values[..., :halves]], axis=-1)
    return values * cosine[:, None, :] + turned * sine[:, None, :]

def piece_index(starts, places):
    labels = jnp.zeros(places.shape, jnp.int32)
    for which in range(2):
        inside = (places >= starts[which]) & (places < starts[which] + PIECE)
        labels = jnp.where(inside, which + 1, labels)
    return labels

def attend(query, keyed, valued, allowed):
    grouped = query.reshape(LEN, KV_HEADS, HEADS // KV_HEADS, HEAD_DIM)
    scores = jnp.einsum('qkrd,skd->krqs', grouped, keyed, precision=highest) * HEAD_DIM ** (-0.5)
    scores = low_back(scores)
    scores = jnp.where(allowed[None, None], scores, -1e+30)
    chances = low(jax.nn.softmax(scores, axis=-1))
    mixed = jnp.einsum('krqs,skd->qkrd', chances, valued, precision=highest)
    return mixed.reshape(LEN, HEADS * HEAD_DIM)

def block_forward(source, places, starts, gain_attn, w_query, w_key, w_value, w_out, gain_mlp, w_gate, w_up, w_down):
    normed = low(source * inverse_rms(source) * gain_attn)
    query = low_back(product(normed, w_query)).reshape(LEN, HEADS, HEAD_DIM)
    keyed = low_back(product(normed, w_key)).reshape(LEN, KV_HEADS, HEAD_DIM)
    valued = low(low_back(product(normed, w_value))).reshape(LEN, KV_HEADS, HEAD_DIM)
    cosine, sine = rope_tables(places)
    query = low(rotate(query, cosine, sine))
    keyed = low(rotate(keyed, cosine, sine))
    tokens_at = jnp.arange(LEN, dtype=jnp.int32)
    labels = piece_index(starts, tokens_at)
    causal = tokens_at[None, :] <= tokens_at[:, None]
    same_piece = (labels[:, None] == labels[None, :]) & (labels[:, None] > 0)
    allowed = causal | same_piece
    mixed = low(low_back(jax.checkpoint(attend)(query, keyed, valued, allowed)))
    middle = source + low_back(product(mixed, w_out.T))
    normed_two = low(middle * inverse_rms(middle) * gain_mlp)
    gated = low_back(product(normed_two, w_gate))
    lifted = low_back(product(normed_two, w_up))
    hidden = low(jax.nn.silu(gated) * lifted)
    return (middle + low_back(product(hidden, w_down.T)), middle)

def reference(layer_input, positions, piece_starts, gain_attn, w_query, w_key, w_value, w_out, gain_mlp, w_gate, w_up, w_down, out_grad):
    params = tuple((item.astype(jnp.float32) for item in (gain_attn, w_query, w_key, w_value, w_out, gain_mlp, w_gate, w_up, w_down)))

    def one_sequence(totals, packed):
        source, places, starts, cotangent = packed
        source = source.astype(jnp.float32)

        def forward(inputs, *weights):
            return block_forward(inputs, places, starts, *weights)
        result, pull, middle = jax.vjp(forward, source, *params, has_aux=True)
        grads = pull(cotangent.astype(jnp.float32))
        totals = tuple((acc + grad for acc, grad in zip(totals, grads[1:])))
        stream = jnp.stack([jnp.sqrt(jnp.mean(source * source)), jnp.sqrt(jnp.mean(middle * middle)), jnp.sqrt(jnp.mean(result * result))])
        return (totals, (result.astype(jnp.bfloat16), grads[0], stream))
    zeros = tuple((jnp.zeros(item.shape, jnp.float32) for item in params))
    totals, (outputs, input_grads, streams) = lax.scan(one_sequence, zeros, (layer_input, positions, piece_starts, out_grad))
    return (outputs, input_grads, totals[0], totals[1], totals[2], totals[3], totals[4], totals[5], totals[6], totals[7], totals[8], streams)
```

```python
import numpy as np

import jax
import jax.numpy as jnp
from jax import lax
from jax.sharding import Mesh, PartitionSpec as P

HEADS = 32
KV_HEADS = 8
HEAD_DIM = 80
PIECE = 256

epsilon = 1e-05
rope_base = 1000000.0

CHIPS = 4
SUM_AXES = ("group", "core", "dp")
REPLICA = ("dp", "chip", "core")


def rope_tables(places):
    halves = HEAD_DIM // 2
    frequency = rope_base ** (-(jnp.arange(halves, dtype=jnp.float32) * 2.0 / HEAD_DIM))
    angles = places.astype(jnp.float32)[..., None] * frequency
    angles = jnp.concatenate([angles, angles], axis=-1)
    return (jnp.cos(angles), jnp.sin(angles))


def rotate(values, cosine, sine):
    halves = HEAD_DIM // 2
    turned = jnp.concatenate([-values[..., halves:], values[..., :halves]], axis=-1)
    return values * cosine[:, None, :] + turned * sine[:, None, :]


def unrotate(grads, cosine, sine):
    halves = HEAD_DIM // 2
    shifted = grads * sine[:, None, :]
    turned = jnp.concatenate([shifted[..., halves:], -shifted[..., :halves]], axis=-1)
    return grads * cosine[:, None, :] + turned


def times(left, right):
    return jnp.dot(left, right, preferred_element_type=jnp.float32)


def times_t(left, right):
    return lax.dot_general(
        left, right, (((1,), (1,)), ((), ())), preferred_element_type=jnp.float32
    )


def inner_t(left, right):
    return lax.dot_general(
        left, right, (((0,), (0,)), ((), ())), preferred_element_type=jnp.float32
    )


def inverse_rms(values):
    return lax.rsqrt(jnp.mean(values * values, axis=-1, keepdims=True) + epsilon)


def norm_back(grad_normed, source, inverse, gain_full):
    weighted = grad_normed * gain_full
    average = jnp.mean(weighted * source, axis=-1, keepdims=True)
    return inverse * weighted - source * (inverse * inverse * inverse) * average


def piece_index(starts, places):
    labels = jnp.zeros(places.shape, jnp.int32)
    for which in range(2):
        inside = (places >= starts[which]) & (places < starts[which] + PIECE)
        labels = jnp.where(inside, which + 1, labels)
    return labels


def swap(value, flip):
    pairs = [(chip, chip ^ flip) for chip in range(CHIPS)]
    return lax.ppermute(value, "chip", pairs)


def collect(block):
    half = block.shape[0] // 2
    first = swap(block, 1)
    second = swap(block, 2)
    low = swap(first[:half], 2)
    high = swap(second[half:], 1)
    return [block, first, second, jnp.concatenate([low, high], axis=0)]


def give_back(parts):
    low_type = jnp.bfloat16
    half = parts[0].shape[0] // 2
    low = swap(parts[3][:half].astype(low_type), 1)
    high = swap(parts[3][half:].astype(low_type), 2)
    for_first = jnp.concatenate(
        [parts[1][:half], parts[1][half:] + high.astype(jnp.float32)], axis=0
    ).astype(low_type)
    for_second = jnp.concatenate(
        [parts[2][:half] + low.astype(jnp.float32), parts[2][half:]], axis=0
    ).astype(low_type)
    from_first = swap(for_first, 1)
    from_second = swap(for_second, 2)
    return parts[0] + from_first.astype(jnp.float32) + from_second.astype(jnp.float32)


def shards(
    layer_input,
    positions,
    piece_starts,
    gain_attn,
    w_query,
    w_key,
    w_value,
    w_out,
    gain_mlp,
    w_gate,
    w_up,
    w_down,
    out_grad,
):
    sequences, block_size, model_width = layer_input.shape
    assert sequences == 1
    groups = lax.axis_size("group")
    spread = lax.axis_size("dp")
    group_at, spread_at = lax.axis_index("group"), lax.axis_index("dp")
    chip, core = lax.axis_index("chip"), lax.axis_index("core")
    full_len = block_size * groups
    scaling = HEAD_DIM ** (-0.5)
    repeats = HEADS // KV_HEADS
    kv_own = KV_HEADS // CHIPS
    heads_own = HEADS // CHIPS
    query_width, kv_width = heads_own * HEAD_DIM, kv_own * HEAD_DIM
    half_rows = w_query.shape[0] // 2

    def own_part(weight):
        width = weight.shape[1] // CHIPS
        return lax.dynamic_slice(weight, (core * half_rows, chip * width), (half_rows, width))

    def gathered(*weights):
        part = jnp.concatenate([own_part(weight) for weight in weights], axis=1)
        return lax.all_gather(part, ("group", "core"), axis=0, tiled=True)

    gains = lax.all_gather(jnp.stack([gain_attn, gain_mlp]), "group", axis=1, tiled=True)
    gain_one, gain_two = gains[0].astype(jnp.float32), gains[1].astype(jnp.float32)

    w_qkv = gathered(w_query, w_key, w_value)
    w_mix = gathered(w_out)
    w_lift = gathered(w_gate, w_up)
    w_sink = gathered(w_down)

    source_low = layer_input[0]
    source_all = jnp.concatenate(collect(source_low), axis=0).astype(jnp.float32)
    small = jnp.concatenate([positions[0], piece_starts[0]])
    smalls = jnp.stack([small, swap(small, 1), swap(small, 2), swap(small, 3)])
    places, starts_all = smalls[:, :block_size].reshape(-1), smalls[:, block_size:]
    grad_low = jnp.concatenate(collect(out_grad[0]), axis=0)

    normed_one = (source_all * inverse_rms(source_all) * gain_one).astype(jnp.bfloat16)
    lin = times(normed_one, w_qkv)
    cosine, sine = rope_tables(places)
    tokens = CHIPS * block_size
    query_rot = rotate(lin[:, :query_width].reshape(tokens, heads_own, HEAD_DIM), cosine, sine)
    query_rot = query_rot.astype(jnp.bfloat16)
    key_rot = rotate(
        lin[:, query_width : query_width + kv_width].reshape(tokens, kv_own, HEAD_DIM), cosine, sine
    ).astype(jnp.bfloat16)
    value_low = lin[:, query_width + kv_width :].astype(jnp.bfloat16)
    both = jnp.concatenate([key_rot.reshape(tokens, kv_width), value_low], axis=1)
    both_all = lax.all_gather(both, "group", axis=0)
    both_all = both_all.reshape(groups, CHIPS, block_size, 2, kv_own, HEAD_DIM)
    both_all = both_all.transpose(3, 1, 4, 0, 2, 5).reshape(2, CHIPS, kv_own, full_len, HEAD_DIM)
    key_all, value_all = both_all[0], both_all[1]

    def by_head(rows):
        rows = rows.reshape(CHIPS, block_size, kv_own, repeats, HEAD_DIM)
        return rows.transpose(0, 2, 3, 1, 4)

    def by_token(heads):
        return heads.transpose(0, 3, 1, 2, 4).reshape(tokens, query_width)

    query_places = group_at * block_size + jnp.arange(block_size, dtype=jnp.int32)
    key_places = jnp.arange(full_len, dtype=jnp.int32)

    def allowed_for(starts):
        query_labels = piece_index(starts, query_places)
        key_labels = piece_index(starts, key_places)
        causal = key_places[None, :] <= query_places[:, None]
        same_piece = (query_labels[:, None] == key_labels[None, :]) & (query_labels[:, None] > 0)
        return causal | same_piece

    query_heads = by_head(query_rot)

    def scores_of(which):
        raw = (
            jnp.einsum(
                "krqd,ksd->krqs",
                query_heads[which],
                key_all[which],
                preferred_element_type=jnp.float32,
            )
            * scaling
        )
        return jnp.where(allowed_for(starts_all[which])[None, None], raw, -1e30)

    mixed_heads, log_totals = [], []
    for which in range(CHIPS):
        masked = scores_of(which)
        highest_score = jnp.max(masked, axis=-1, keepdims=True)
        raised = jnp.exp(masked - highest_score)
        summed = jnp.sum(raised, axis=-1, keepdims=True)
        chances_low = (raised / summed).astype(jnp.bfloat16)
        mixed_heads.append(
            jnp.einsum(
                "krqs,ksd->krqd",
                chances_low,
                value_all[which],
                preferred_element_type=jnp.float32,
            ).astype(jnp.bfloat16)
        )
        log_totals.append(highest_score + jnp.log(summed))
    mixed_low = by_token(jnp.stack(mixed_heads))

    def blocks_of(values):
        return [values[i * block_size : (i + 1) * block_size] for i in range(CHIPS)]

    source = source_low.astype(jnp.float32)
    inverse_one = inverse_rms(source)
    unit_one = source * inverse_one
    middle = source + give_back(blocks_of(times_t(mixed_low, w_mix)))
    inverse_two = inverse_rms(middle)
    unit_two = middle * inverse_two
    normed_two = jnp.concatenate(collect((unit_two * gain_two).astype(jnp.bfloat16)), axis=0)
    wide = w_lift.shape[1] // 2
    both_up = times(normed_two, w_lift)
    gated, lifted = both_up[:, :wide], both_up[:, wide:]
    activated = jax.nn.silu(gated)
    hidden = (activated * lifted).astype(jnp.bfloat16)
    output_full = middle + give_back(blocks_of(times_t(hidden, w_sink)))

    grad_hidden = times(grad_low, w_sink)
    sigmoid_gate = jax.nn.sigmoid(gated)
    grad_gate_low = (
        grad_hidden * lifted * (sigmoid_gate + gated * sigmoid_gate * (1.0 - sigmoid_gate))
    ).astype(jnp.bfloat16)
    grad_lift_low = (grad_hidden * activated).astype(jnp.bfloat16)
    grad_both = jnp.concatenate([grad_gate_low, grad_lift_low], axis=1)
    grad_normed_two = give_back(blocks_of(times_t(grad_both, w_lift)))
    grad_gain_two = jnp.sum(grad_normed_two * unit_two, axis=0)
    grad_middle = out_grad[0].astype(jnp.float32) + norm_back(
        grad_normed_two, middle, inverse_two, gain_two
    )
    grad_middle_low = jnp.concatenate(collect(grad_middle.astype(jnp.bfloat16)), axis=0)
    grad_mixed_low = by_head(times(grad_middle_low, w_mix).astype(jnp.bfloat16))

    grad_query_heads, grad_keys, grad_values = [], [], []
    for which in range(CHIPS):
        chances = jnp.exp(scores_of(which) - log_totals[which])
        grad_seq = grad_mixed_low[which]
        grad_values.append(
            jnp.einsum(
                "krqs,krqd->ksd",
                chances.astype(jnp.bfloat16),
                grad_seq,
                preferred_element_type=jnp.float32,
            )
        )
        grad_chance = jnp.einsum(
            "krqd,ksd->krqs", grad_seq, value_all[which], preferred_element_type=jnp.float32
        )
        grad_score = chances * (
            grad_chance - jnp.sum(chances * grad_chance, axis=-1, keepdims=True)
        )
        grad_score = grad_score.astype(jnp.bfloat16)
        grad_query_heads.append(
            jnp.einsum(
                "krqs,ksd->krqd", grad_score, key_all[which], preferred_element_type=jnp.float32
            )
            * scaling
        )
        grad_keys.append(
            jnp.einsum(
                "krqs,krqd->ksd",
                grad_score,
                query_heads[which],
                preferred_element_type=jnp.float32,
            )
            * scaling
        )
    grad_kv = jnp.stack([jnp.stack(grad_keys), jnp.stack(grad_values)]).astype(jnp.bfloat16)
    grad_kv = grad_kv.reshape(2, CHIPS, kv_own, groups, block_size, HEAD_DIM)
    grad_kv = grad_kv.transpose(3, 1, 4, 0, 2, 5).reshape(groups * tokens, 2 * kv_width)
    grad_kv = lax.psum_scatter(grad_kv, "group", scatter_dimension=0, tiled=True)
    grad_query_low = unrotate(
        by_token(jnp.stack(grad_query_heads)).reshape(tokens, heads_own, HEAD_DIM), cosine, sine
    ).astype(jnp.bfloat16)
    grad_key_low = unrotate(
        grad_kv[:, :kv_width].astype(jnp.float32).reshape(tokens, kv_own, HEAD_DIM), cosine, sine
    ).astype(jnp.bfloat16)
    grad_qkv = jnp.concatenate(
        [
            grad_query_low.reshape(tokens, query_width),
            grad_key_low.reshape(tokens, kv_width),
            grad_kv[:, kv_width:],
        ],
        axis=1,
    )
    added = give_back(blocks_of(times_t(grad_qkv, w_qkv)))
    grad_gain_one = jnp.sum(added * unit_one, axis=0)
    input_grad = grad_middle + norm_back(added, source, inverse_one, gain_one)

    count = spread * CHIPS * 2
    whose = (spread_at * CHIPS + chip) * 2 + core

    def owned(left, right, widths):
        total = inner_t(left, right).astype(jnp.bfloat16)
        total = lax.psum_scatter(total, SUM_AXES, scatter_dimension=0, tiled=True)
        rows, columns = total.shape[0] // CHIPS, total.shape[1]
        total = total.reshape(CHIPS, rows, columns)
        pieces = []
        for step in range(CHIPS):
            pairs = []
            for source_at in range(count):
                at_spread, at_chip, at_core = (
                    source_at // (2 * CHIPS),
                    source_at // 2 % CHIPS,
                    source_at % 2,
                )
                target = (at_core * spread + at_spread) * CHIPS + (at_chip ^ step)
                pairs.append((source_at, target))
            block = lax.dynamic_index_in_dim(total, chip ^ step, axis=0, keepdims=False)
            pieces.append(lax.ppermute(block, REPLICA, pairs))
        pieces = jnp.stack(pieces)
        ordered = [
            lax.dynamic_index_in_dim(pieces, (whose % CHIPS) ^ at, axis=0, keepdims=False)
            for at in range(CHIPS)
        ]
        result, start = [], 0
        for width in widths:
            result.append(
                jnp.concatenate([part[:, start : start + width] for part in ordered], axis=1)
            )
            start += width
        return [item.astype(jnp.float32) for item in result]

    (grad_down,) = owned(grad_low, hidden, (wide,))
    grad_gate, grad_up = owned(normed_two, grad_both, (wide, wide))
    (grad_out,) = owned(grad_middle_low, mixed_low, (query_width,))
    grad_query, grad_key, grad_value = owned(
        normed_one, grad_qkv, (query_width, kv_width, kv_width)
    )

    gain_owned = lax.psum_scatter(
        jnp.stack([grad_gain_one, grad_gain_two]),
        ("group",) + REPLICA,
        scatter_dimension=1,
        tiled=True,
    )
    squares = jnp.stack(
        [jnp.sum(source * source), jnp.sum(middle * middle), jnp.sum(output_full * output_full)]
    )
    square_totals = lax.psum(squares[None], "group")
    stream_rms = jnp.sqrt(square_totals / (full_len * model_width))
    return (
        output_full.astype(jnp.bfloat16)[None],
        input_grad[None],
        gain_owned[0],
        grad_query,
        grad_key,
        grad_value,
        grad_out,
        gain_owned[1],
        grad_gate,
        grad_up,
        grad_down,
        stream_rms,
    )


def solution(mesh):
    groups, replicas = mesh.shape["group"], mesh.shape["replica"]
    spread = replicas // (2 * CHIPS)
    devices = np.asarray(mesh.devices).reshape(groups, spread, CHIPS, 2)
    split = Mesh(devices, ("group", "dp", "chip", "core"))
    everyone = ("group",) + REPLICA
    placed = (
        P(REPLICA, "group", None),
        P(REPLICA, "group"),
        P(REPLICA, None),
        P("group"),
        P("group", None),
        P("group", None),
        P("group", None),
        P("group", None),
        P("group"),
        P("group", None),
        P("group", None),
        P("group", None),
        P(REPLICA, "group", None),
    )
    return jax.shard_map(
        shards,
        mesh=split,
        in_specs=placed,
        out_specs=(
            P(REPLICA, "group", None),
            P(REPLICA, "group", None),
            P(everyone),
            P(everyone, None),
            P(everyone, None),
            P(everyone, None),
            P(everyone, None),
            P(everyone),
            P(everyone, None),
            P(everyone, None),
            P(everyone, None),
            P(REPLICA, None),
        ),
        check_vma=False,
    )
```

```python
import numpy as np

import jax
import jax.numpy as jnp
from jax import lax
from jax.experimental import pallas as pl
from jax.experimental.pallas import tpu as pltpu
from jax.experimental.layout import Layout, with_layout_constraint
from jax.sharding import Mesh, PartitionSpec as P

HEADS = 32
KV_HEADS = 8
HEAD_DIM = 80
PIECE = 256

epsilon = 1e-05
rope_base = 1000000.0

CHIPS = 4
SUM_AXES = ("group", "core", "dp")
REPLICA = ("dp", "chip", "core")


HALF = HEAD_DIM // 2
LOG2E = 1.4426950408889634


def rope_tables(places):
    frequency = rope_base ** (-(jnp.arange(HALF, dtype=jnp.float32) * 2.0 / HEAD_DIM))
    angles = frequency[:, None] * places.astype(jnp.float32)[None, :]
    return (jnp.cos(angles), jnp.sin(angles))


def rotate(values, cosine, sine):
    first, second = halves_of(values)
    return joined(first * cosine - second * sine, second * cosine + first * sine)


def unrotate(grads, cosine, sine):
    first, second = halves_of(grads)
    return joined(first * cosine + second * sine, second * cosine - first * sine)


def halves_of(values):
    heads = values.reshape(-1, 2, HALF, values.shape[-1])
    return heads[:, 0], heads[:, 1]


def joined(first, second):
    return jnp.stack([first, second], axis=1).reshape(-1, first.shape[-1])


def flipped(values):
    return values.astype(jnp.float32).T.astype(jnp.bfloat16)


def attend_kernel(repeats, query_ref, kv_ref, limit_ref, mixed_ref, total_ref, out_ref):
    groups, kv_rows, block = kv_ref.shape
    kv_width = kv_rows // 2
    factor = HEAD_DIM ** (-0.5) * LOG2E
    key_at = lax.broadcasted_iota(jnp.int32, (block, block), 0)
    limits = limit_ref[0]
    for kv in range(kv_width // HEAD_DIM):
        rows = slice(kv * HEAD_DIM, (kv + 1) * HEAD_DIM)
        value_rows = slice(kv_width + kv * HEAD_DIM, kv_width + (kv + 1) * HEAD_DIM)
        keys = [flipped(kv_ref[group, rows, :]) for group in range(groups)]
        for head in range(kv * repeats, (kv + 1) * repeats):
            head_rows = slice(head * HEAD_DIM, (head + 1) * HEAD_DIM)
            query = query_ref[head_rows, :]
            scores = []
            for group in range(groups):
                raw = jnp.dot(keys[group], query, preferred_element_type=jnp.float32)
                scores.append(jnp.where(key_at < limits - group * block, raw, -1e30))
            highest = scores[0]
            for group in range(1, groups):
                highest = jnp.maximum(highest, scores[group])
            highest = jnp.max(highest, axis=0, keepdims=True) * factor
            row_sum, mixed = None, None
            for group in range(groups):
                raised = jnp.exp2(scores[group] * factor - highest)
                part_sum = jnp.sum(raised, axis=0, keepdims=True)
                part = jnp.dot(
                    kv_ref[group, value_rows, :],
                    raised.astype(jnp.bfloat16),
                    preferred_element_type=jnp.float32,
                )
                row_sum = part_sum if row_sum is None else row_sum + part_sum
                mixed = part if mixed is None else mixed + part
            out_ref[head_rows, :] = mixed / row_sum
            total_ref[0, head : head + 1, :] = highest + jnp.log2(row_sum)
    mixed_ref[...] = out_ref[...].T.astype(jnp.bfloat16)


def attend(query, kv_all, limits, repeats):
    query_width, tokens = query.shape
    groups, kv_rows, _ = kv_all.shape
    chips, _, block = limits.shape
    heads = query_width // HEAD_DIM
    pairs = query_width * tokens * groups * block
    return pl.pallas_call(
        lambda *refs: attend_kernel(repeats, *refs),
        out_shape=(
            jax.ShapeDtypeStruct((tokens, query_width), jnp.bfloat16),
            jax.ShapeDtypeStruct((chips, heads, block), jnp.float32),
        ),
        grid=(chips,),
        in_specs=[
            pl.BlockSpec((query_width, block), lambda i: (0, i)),
            pl.BlockSpec((groups, kv_rows, block), lambda i: (0, 0, i)),
            pl.BlockSpec((1, 1, block), lambda i: (i, 0, 0)),
        ],
        out_specs=(
            pl.BlockSpec((block, query_width), lambda i: (i, 0)),
            pl.BlockSpec((1, heads, block), lambda i: (i, 0, 0)),
        ),
        scratch_shapes=[pltpu.VMEM((query_width, block), jnp.float32)],
        cost_estimate=pl.CostEstimate(
            flops=4 * pairs,
            bytes_accessed=2 * (2 * query.size + kv_all.size),
            transcendentals=pairs // HEAD_DIM,
        ),
        name="attend",
    )(query, kv_all, limits)


def attend_back_kernel(
    repeats,
    query_ref,
    kv_ref,
    limit_ref,
    total_ref,
    mixed_ref,
    grad_ref,
    cosine_ref,
    sine_ref,
    grad_query_ref,
    grad_kv_ref,
    grad_rows_ref,
    mixed_rows_ref,
    query_rows_ref,
    key_sum_ref,
    value_sum_ref,
):
    groups, kv_rows, block = kv_ref.shape
    kv_width = kv_rows // 2
    scaling = HEAD_DIM ** (-0.5)
    factor = scaling * LOG2E
    key_at = lax.broadcasted_iota(jnp.int32, (block, block), 0)
    limits = limit_ref[0]
    cosine, sine = cosine_ref[...], sine_ref[...]
    grad_rows_ref[...] = grad_ref[...].astype(jnp.float32).T
    mixed_rows_ref[...] = mixed_ref[...].astype(jnp.float32).T
    for kv in range(kv_width // HEAD_DIM):
        rows = slice(kv * HEAD_DIM, (kv + 1) * HEAD_DIM)
        value_rows = slice(kv_width + kv * HEAD_DIM, kv_width + (kv + 1) * HEAD_DIM)
        keys = [flipped(kv_ref[group, rows, :]) for group in range(groups)]
        values = [flipped(kv_ref[group, value_rows, :]) for group in range(groups)]
        for step in range(repeats):
            head = kv * repeats + step
            head_rows = slice(head * HEAD_DIM, (head + 1) * HEAD_DIM)
            query = query_ref[head_rows, :]
            query_tokens = flipped(query)
            grads = grad_rows_ref[head_rows, :]
            delta = jnp.sum(grads * mixed_rows_ref[head_rows, :], axis=0, keepdims=True)
            grads_low = grads.astype(jnp.bfloat16)
            grad_tokens = grads.T.astype(jnp.bfloat16)
            total = total_ref[0, head : head + 1, :]
            grad_query = None
            for group in range(groups):
                raw = jnp.dot(keys[group], query, preferred_element_type=jnp.float32)
                chances = jnp.where(
                    key_at < limits - group * block, jnp.exp2(raw * factor - total), 0.0
                )
                grad_chance = jnp.dot(
                    values[group], grads_low, preferred_element_type=jnp.float32
                )
                grad_score = (chances * (grad_chance - delta)).astype(jnp.bfloat16)
                part = jnp.dot(
                    kv_ref[group, rows, :], grad_score, preferred_element_type=jnp.float32
                )
                grad_query = part if grad_query is None else grad_query + part
                key_part = jnp.dot(
                    grad_score, query_tokens, preferred_element_type=jnp.float32
                )
                value_part = jnp.dot(
                    chances.astype(jnp.bfloat16), grad_tokens, preferred_element_type=jnp.float32
                )
                if step == 0:
                    key_sum_ref[group] = key_part
                    value_sum_ref[group] = value_part
                else:
                    key_sum_ref[group] += key_part
                    value_sum_ref[group] += value_part
            first, second = grad_query[:HALF] * scaling, grad_query[HALF:] * scaling
            query_rows_ref[head * HEAD_DIM : head * HEAD_DIM + HALF, :] = (
                first * cosine + second * sine
            )
            query_rows_ref[head * HEAD_DIM + HALF : (head + 1) * HEAD_DIM, :] = (
                second * cosine - first * sine
            )
        for group in range(groups):
            grad_kv_ref[group, rows, :] = (key_sum_ref[group].T * scaling).astype(jnp.bfloat16)
            grad_kv_ref[group, value_rows, :] = value_sum_ref[group].T.astype(jnp.bfloat16)
    grad_query_ref[...] = query_rows_ref[...].T.astype(jnp.bfloat16)


def attend_back(query, kv_all, limits, totals, mixed, grad_mixed, cosine, sine, repeats):
    query_width, tokens = query.shape
    groups, kv_rows, _ = kv_all.shape
    chips, _, block = limits.shape
    heads = query_width // HEAD_DIM
    pairs = query_width * tokens * groups * block
    by_column = pl.BlockSpec((query_width, block), lambda i: (0, i))
    by_row = pl.BlockSpec((block, query_width), lambda i: (i, 0))
    by_key = pl.BlockSpec((groups, kv_rows, block), lambda i: (0, 0, i))
    table = pl.BlockSpec((HALF, block), lambda i: (0, i))
    return pl.pallas_call(
        lambda *refs: attend_back_kernel(repeats, *refs),
        out_shape=(
            jax.ShapeDtypeStruct((tokens, query_width), jnp.bfloat16),
            jax.ShapeDtypeStruct(kv_all.shape, jnp.bfloat16),
        ),
        grid=(chips,),
        in_specs=[
            by_column,
            by_key,
            pl.BlockSpec((1, 1, block), lambda i: (i, 0, 0)),
            pl.BlockSpec((1, heads, block), lambda i: (i, 0, 0)),
            by_row,
            by_row,
            table,
            table,
        ],
        out_specs=(by_row, by_key),
        scratch_shapes=[
            pltpu.VMEM((query_width, block), jnp.float32),
            pltpu.VMEM((query_width, block), jnp.float32),
            pltpu.VMEM((query_width, block), jnp.float32),
            pltpu.VMEM((groups, block, HEAD_DIM), jnp.float32),
            pltpu.VMEM((groups, block, HEAD_DIM), jnp.float32),
        ],
        cost_estimate=pl.CostEstimate(
            flops=10 * pairs,
            bytes_accessed=2 * (4 * query.size + 2 * kv_all.size),
            transcendentals=pairs // HEAD_DIM,
        ),
        name="attend_back",
    )(query, kv_all, limits, totals, mixed, grad_mixed, cosine, sine)


def times(left, right):
    return jnp.dot(left, right, preferred_element_type=jnp.float32)


def times_t(left, right):
    return lax.dot_general(
        left, right, (((1,), (1,)), ((), ())), preferred_element_type=jnp.float32
    )


def inner_t(left, right):
    return lax.dot_general(
        left, right, (((0,), (0,)), ((), ())), preferred_element_type=jnp.float32
    )


def inverse_rms(values):
    return lax.rsqrt(jnp.mean(values * values, axis=-1, keepdims=True) + epsilon)


def norm_back(grad_normed, source, inverse, gain_full):
    weighted = grad_normed * gain_full
    average = jnp.mean(weighted * source, axis=-1, keepdims=True)
    return inverse * weighted - source * (inverse * inverse * inverse) * average


def limits_of(starts, places):
    limits = places + 1
    for which in range(2):
        inside = (places >= starts[which]) & (places < starts[which] + PIECE)
        limits = jnp.where(inside, starts[which] + PIECE, limits)
    return limits


def swap(value, flip):
    pairs = [(chip, chip ^ flip) for chip in range(CHIPS)]
    return lax.ppermute(value, "chip", pairs)


def collect(block):
    half = block.shape[0] // 2
    first = swap(block, 1)
    second = swap(block, 2)
    low = swap(first[:half], 2)
    high = swap(second[half:], 1)
    return [block, first, second, jnp.concatenate([low, high], axis=0)]


def give_back(total):
    low_type, wide_type = jnp.bfloat16, jnp.float32
    own, first, second, third = jnp.split(total, CHIPS)
    half = own.shape[0] // 2
    low = swap(third[:half], 1).astype(wide_type)
    high = swap(third[half:], 2).astype(wide_type)
    for_first = jnp.concatenate(
        [first[:half], (first[half:].astype(wide_type) + high).astype(low_type)], axis=0
    )
    for_second = jnp.concatenate(
        [(second[:half].astype(wide_type) + low).astype(low_type), second[half:]], axis=0
    )
    from_first = swap(for_first, 1).astype(wide_type)
    from_second = swap(for_second, 2).astype(wide_type)
    return own.astype(wide_type) + from_first + from_second


def shards(
    layer_input,
    positions,
    piece_starts,
    gain_attn,
    w_query,
    w_key,
    w_value,
    w_out,
    gain_mlp,
    w_gate,
    w_up,
    w_down,
    out_grad,
):
    sequences, block_size, model_width = layer_input.shape
    assert sequences == 1
    groups = lax.axis_size("group")
    spread = lax.axis_size("dp")
    group_at, spread_at = lax.axis_index("group"), lax.axis_index("dp")
    chip, core = lax.axis_index("chip"), lax.axis_index("core")
    full_len = block_size * groups
    scaling = HEAD_DIM ** (-0.5)
    repeats = HEADS // KV_HEADS
    kv_own = KV_HEADS // CHIPS
    heads_own = HEADS // CHIPS
    query_width, kv_width = heads_own * HEAD_DIM, kv_own * HEAD_DIM
    half_rows = w_query.shape[0] // 2

    def own_part(weight):
        width = weight.shape[1] // CHIPS
        return lax.dynamic_slice(weight, (core * half_rows, chip * width), (half_rows, width))

    def gathered(*weights):
        part = jnp.concatenate([own_part(weight) for weight in weights], axis=1)
        return lax.all_gather(part, ("group", "core"), axis=0, tiled=True)

    gains = lax.all_gather(jnp.stack([gain_attn, gain_mlp]), "group", axis=1, tiled=True)
    gain_one, gain_two = gains[0].astype(jnp.float32), gains[1].astype(jnp.float32)

    w_attn = gathered(w_query, w_key, w_value, w_out)
    w_qkv, w_mix = w_attn[:, :-query_width], w_attn[:, -query_width:]
    w_lift = gathered(w_gate, w_up)
    w_sink = gathered(w_down)

    source_low = layer_input[0]
    source_all = jnp.concatenate(collect(source_low), axis=0).astype(jnp.float32)
    small = jnp.concatenate([positions[0], piece_starts[0]])
    smalls = jnp.stack([small, swap(small, 1), swap(small, 2), swap(small, 3)])
    places, starts_all = smalls[:, :block_size].reshape(-1), smalls[:, block_size:]
    grad_low = jnp.concatenate(collect(out_grad[0]), axis=0)

    normed_one = (source_all * inverse_rms(source_all) * gain_one).astype(jnp.bfloat16)
    cosine, sine = rope_tables(places)
    tokens = CHIPS * block_size
    lin = lax.dot_general(
        w_qkv, normed_one, (((0,), (1,)), ((), ())), preferred_element_type=jnp.float32
    )
    query_rot = rotate(lin[:query_width], cosine, sine).astype(jnp.bfloat16)
    key_rot = rotate(lin[query_width : query_width + kv_width], cosine, sine)
    kv_own_tokens = jnp.concatenate(
        [key_rot.astype(jnp.bfloat16), lin[query_width + kv_width :].astype(jnp.bfloat16)], axis=0
    )
    kv_all = lax.all_gather(kv_own_tokens, "group", axis=0, tiled=True)
    kv_all = kv_all.reshape(groups, 2 * kv_width, tokens)

    def reduced(total):
        return lax.psum_scatter(total, SUM_AXES, scatter_dimension=0, tiled=True)

    def product_low(left, right):
        return inner_t(left, right).astype(jnp.bfloat16)

    then = lax.optimization_barrier

    count = spread * CHIPS * 2
    whose = (spread_at * CHIPS + chip) * 2 + core

    def owned(total):
        rows, columns = total.shape[0] // CHIPS, total.shape[1]
        total = total.reshape(CHIPS, rows, columns)
        pieces = []
        for step in range(CHIPS):
            pairs = []
            for source_at in range(count):
                at_spread, at_chip, at_core = (
                    source_at // (2 * CHIPS),
                    source_at // 2 % CHIPS,
                    source_at % 2,
                )
                target = (at_core * spread + at_spread) * CHIPS + (at_chip ^ step)
                pairs.append((source_at, target))
            block = lax.dynamic_index_in_dim(total, chip ^ step, axis=0, keepdims=False)
            pieces.append(lax.ppermute(block, REPLICA, pairs))
        pieces = jnp.stack(pieces)
        return [
            lax.dynamic_index_in_dim(pieces, (whose % CHIPS) ^ at, axis=0, keepdims=False)
            for at in range(CHIPS)
        ]

    def laid(parts, start, width):
        parts = [part[:, start : start + width] for part in parts]
        return jnp.concatenate(parts, axis=1).astype(jnp.float32)

    query_places = group_at * block_size + jnp.arange(block_size, dtype=jnp.int32)
    limits = jnp.stack([limits_of(starts_all[which], query_places) for which in range(CHIPS)])
    limits = limits[:, None, :]
    mixed_low, log_totals = attend(query_rot, kv_all, limits, repeats)

    def parts(left, right):
        return times_t(left, right).astype(jnp.bfloat16)

    source = source_low.astype(jnp.float32)
    inverse_one = inverse_rms(source)
    unit_one = source * inverse_one
    middle = source + give_back(parts(mixed_low, w_mix))
    inverse_two = inverse_rms(middle)
    unit_two = middle * inverse_two
    normed_two = jnp.concatenate(collect((unit_two * gain_two).astype(jnp.bfloat16)), axis=0)
    wide = w_lift.shape[1] // 2
    both_up = times(normed_two, w_lift)
    gated, lifted = both_up[:, :wide], both_up[:, wide:]
    activated = jax.nn.silu(gated)
    hidden = (activated * lifted).astype(jnp.bfloat16)
    total_down, w_sink = then((product_low(grad_low, hidden), w_sink))
    sum_down = reduced(total_down)

    grad_hidden = times(grad_low, w_sink)
    sigmoid_gate = jax.nn.sigmoid(gated)
    grad_gate_low = (
        grad_hidden * lifted * (sigmoid_gate + gated * sigmoid_gate * (1.0 - sigmoid_gate))
    ).astype(jnp.bfloat16)
    grad_lift_low = (grad_hidden * activated).astype(jnp.bfloat16)
    grad_both = jnp.concatenate([grad_gate_low, grad_lift_low], axis=1)
    grad_parts, grad_both = then((parts(grad_both, w_lift), grad_both))
    sum_lift = reduced(product_low(normed_two, grad_both))
    grad_normed_two = give_back(grad_parts)
    grad_normed_two, sum_down = then((grad_normed_two, sum_down))
    grad_gain_two = jnp.sum(grad_normed_two * unit_two, axis=0)
    grad_middle = out_grad[0].astype(jnp.float32) + norm_back(
        grad_normed_two, middle, inverse_two, gain_two
    )
    hidden, grad_middle = then((hidden, grad_middle))
    grad_middle_low = jnp.concatenate(collect(grad_middle.astype(jnp.bfloat16)), axis=0)
    sink_parts, grad_middle_low = then((parts(hidden, w_sink), grad_middle_low))
    output_full = middle + give_back(sink_parts)
    grad_mixed_low = times(grad_middle_low, w_mix).astype(jnp.bfloat16)
    grad_query_low, grad_kv = attend_back(
        query_rot, kv_all, limits, log_totals, mixed_low, grad_mixed_low, cosine, sine, repeats
    )
    grad_kv, sum_lift = then((grad_kv.reshape(groups * 2 * kv_width, tokens), sum_lift))
    grad_kv = lax.psum_scatter(grad_kv, "group", scatter_dimension=0, tiled=True)
    grad_down = laid(owned(sum_down), 0, wide)
    lift_parts = owned(sum_lift)
    grad_gate, grad_up = laid(lift_parts, 0, wide), laid(lift_parts, wide, wide)
    grad_kv, lift_parts, output_full = then((grad_kv, lift_parts, output_full))
    grad_key = unrotate(grad_kv[:kv_width].astype(jnp.float32), cosine, sine)
    grad_kv_low = jnp.concatenate([grad_key.astype(jnp.bfloat16), grad_kv[kv_width:]], axis=0).T
    total_query = product_low(normed_one, grad_query_low)
    total_out = product_low(grad_middle_low, mixed_low)
    both_totals = with_layout_constraint(
        jnp.concatenate([total_query, total_out], axis=1), Layout(major_to_minor=(0, 1))
    )
    both_totals, grad_kv_low = then((both_totals, grad_kv_low))
    both_sums = reduced(both_totals)
    added_query = times_t(grad_query_low, w_qkv[:, :query_width])
    added = added_query + times_t(grad_kv_low, w_qkv[:, query_width:])
    added = give_back(added.astype(jnp.bfloat16))
    grad_gain_one = jnp.sum(added * unit_one, axis=0)
    input_grad = grad_middle + norm_back(added, source, inverse_one, gain_one)
    squares = jnp.stack(
        [jnp.sum(source * source), jnp.sum(middle * middle), jnp.sum(output_full * output_full)]
    )
    place = core * spread + spread_at
    apart = jnp.where(jnp.arange(2 * spread)[:, None] == place, squares[None, :], 0.0)
    apart = apart.reshape(1, -1)
    extra = jnp.concatenate(
        [
            grad_gain_one[:, None],
            grad_gain_two[:, None],
            jnp.broadcast_to(apart, (model_width, apart.shape[1])),
        ],
        axis=1,
    ).astype(jnp.bfloat16)
    kv_totals = jnp.concatenate([product_low(normed_one, grad_kv_low), extra], axis=1)
    kv_totals, both_sums = then((kv_totals, both_sums))
    kv_sums = reduced(kv_totals)
    square_totals = lax.dynamic_slice(
        kv_sums[:1, 2 * kv_width + 2 :].astype(jnp.float32), (0, place * 3), (1, 3)
    )
    stream_rms = jnp.sqrt(square_totals / (full_len * model_width))

    both_parts = owned(both_sums)
    grad_query = laid(both_parts, 0, query_width)
    grad_out = laid(both_parts, query_width, query_width)
    kv_parts = owned(kv_sums[:, : 2 * kv_width + 2])
    grad_key, grad_value = laid(kv_parts, 0, kv_width), laid(kv_parts, kv_width, kv_width)
    gains_owned = sum(part[:, 2 * kv_width :].astype(jnp.float32) for part in kv_parts)

    return (
        output_full.astype(jnp.bfloat16)[None],
        input_grad[None],
        gains_owned[:, 0],
        grad_query,
        grad_key,
        grad_value,
        grad_out,
        gains_owned[:, 1],
        grad_gate,
        grad_up,
        grad_down,
        stream_rms,
    )


def solution(mesh):
    groups, replicas = mesh.shape["group"], mesh.shape["replica"]
    spread = replicas // (2 * CHIPS)
    devices = np.asarray(mesh.devices).reshape(groups, spread, CHIPS, 2)
    split = Mesh(devices, ("group", "dp", "chip", "core"))
    everyone = ("group",) + REPLICA
    placed = (
        P(REPLICA, "group", None),
        P(REPLICA, "group"),
        P(REPLICA, None),
        P("group"),
        P("group", None),
        P("group", None),
        P("group", None),
        P("group", None),
        P("group"),
        P("group", None),
        P("group", None),
        P("group", None),
        P(REPLICA, "group", None),
    )
    return jax.shard_map(
        shards,
        mesh=split,
        in_specs=placed,
        out_specs=(
            P(REPLICA, "group", None),
            P(REPLICA, "group", None),
            P(everyone),
            P(everyone, None),
            P(everyone, None),
            P(everyone, None),
            P(everyone, None),
            P(everyone),
            P(everyone, None),
            P(everyone, None),
            P(everyone, None),
            P(REPLICA, None),
        ),
        check_vma=False,
    )
```

```python
import numpy as np

import jax
import jax.numpy as jnp
from jax import lax
from jax.experimental import pallas as pl
from jax.experimental.pallas import tpu as pltpu
from jax.experimental.layout import Layout, with_layout_constraint
from jax.sharding import Mesh, PartitionSpec as P

HEADS = 32
KV_HEADS = 8
HEAD_DIM = 80
PIECE = 256

epsilon = 1e-05
rope_base = 1000000.0

CHIPS = 4
SUM_AXES = ("group", "core", "dp")
REPLICA = ("dp", "chip", "core")


HALF = HEAD_DIM // 2
LOG2E = 1.4426950408889634


def rope_tables(places):
    frequency = rope_base ** (-(jnp.arange(HALF, dtype=jnp.float32) * 2.0 / HEAD_DIM))
    angles = frequency[:, None] * places.astype(jnp.float32)[None, :]
    return (jnp.cos(angles), jnp.sin(angles))


def rotate(values, cosine, sine):
    first, second = halves_of(values)
    return joined(first * cosine - second * sine, second * cosine + first * sine)


def unrotate(grads, cosine, sine):
    first, second = halves_of(grads)
    return joined(first * cosine + second * sine, second * cosine - first * sine)


def halves_of(values):
    heads = values.reshape(-1, 2, HALF, values.shape[-1])
    return heads[:, 0], heads[:, 1]


def joined(first, second):
    return jnp.stack([first, second], axis=1).reshape(-1, first.shape[-1])


def flipped(values):
    return values.astype(jnp.float32).T.astype(jnp.bfloat16)


def attend_kernel(repeats, query_ref, kv_ref, limit_ref, mixed_ref, total_ref, out_ref):
    groups, kv_rows, block = kv_ref.shape
    kv_width = kv_rows // 2
    factor = HEAD_DIM ** (-0.5) * LOG2E
    key_at = lax.broadcasted_iota(jnp.int32, (block, block), 0)
    limits = limit_ref[0]
    for kv in range(kv_width // HEAD_DIM):
        rows = slice(kv * HEAD_DIM, (kv + 1) * HEAD_DIM)
        value_rows = slice(kv_width + kv * HEAD_DIM, kv_width + (kv + 1) * HEAD_DIM)
        keys = [flipped(kv_ref[group, rows, :]) for group in range(groups)]
        for head in range(kv * repeats, (kv + 1) * repeats):
            head_rows = slice(head * HEAD_DIM, (head + 1) * HEAD_DIM)
            query = query_ref[head_rows, :]
            scores = []
            for group in range(groups):
                raw = jnp.dot(keys[group], query, preferred_element_type=jnp.float32)
                scores.append(jnp.where(key_at < limits - group * block, raw, -1e30))
            highest = scores[0]
            for group in range(1, groups):
                highest = jnp.maximum(highest, scores[group])
            highest = jnp.max(highest, axis=0, keepdims=True) * factor
            row_sum, mixed = None, None
            for group in range(groups):
                raised = jnp.exp2(scores[group] * factor - highest)
                part_sum = jnp.sum(raised, axis=0, keepdims=True)
                part = jnp.dot(
                    kv_ref[group, value_rows, :],
                    raised.astype(jnp.bfloat16),
                    preferred_element_type=jnp.float32,
                )
                row_sum = part_sum if row_sum is None else row_sum + part_sum
                mixed = part if mixed is None else mixed + part
            out_ref[head_rows, :] = mixed / row_sum
            total_ref[0, head : head + 1, :] = highest + jnp.log2(row_sum)
    mixed_ref[...] = out_ref[...].T.astype(jnp.bfloat16)


def attend(query, kv_all, limits, repeats):
    query_width, tokens = query.shape
    groups, kv_rows, _ = kv_all.shape
    chips, _, block = limits.shape
    heads = query_width // HEAD_DIM
    pairs = query_width * tokens * groups * block
    return pl.pallas_call(
        lambda *refs: attend_kernel(repeats, *refs),
        out_shape=(
            jax.ShapeDtypeStruct((tokens, query_width), jnp.bfloat16),
            jax.ShapeDtypeStruct((chips, heads, block), jnp.float32),
        ),
        grid=(chips,),
        in_specs=[
            pl.BlockSpec((query_width, block), lambda i: (0, i)),
            pl.BlockSpec((groups, kv_rows, block), lambda i: (0, 0, i)),
            pl.BlockSpec((1, 1, block), lambda i: (i, 0, 0)),
        ],
        out_specs=(
            pl.BlockSpec((block, query_width), lambda i: (i, 0)),
            pl.BlockSpec((1, heads, block), lambda i: (i, 0, 0)),
        ),
        scratch_shapes=[pltpu.VMEM((query_width, block), jnp.float32)],
        cost_estimate=pl.CostEstimate(
            flops=4 * pairs,
            bytes_accessed=2 * (2 * query.size + kv_all.size),
            transcendentals=pairs // HEAD_DIM,
        ),
        name="attend",
    )(query, kv_all, limits)


def attend_back_kernel(
    repeats,
    query_ref,
    kv_ref,
    limit_ref,
    total_ref,
    mixed_ref,
    grad_ref,
    cosine_ref,
    sine_ref,
    grad_query_ref,
    grad_kv_ref,
    grad_rows_ref,
    mixed_rows_ref,
    query_rows_ref,
    key_sum_ref,
    value_sum_ref,
):
    groups, kv_rows, block = kv_ref.shape
    kv_width = kv_rows // 2
    scaling = HEAD_DIM ** (-0.5)
    factor = scaling * LOG2E
    key_at = lax.broadcasted_iota(jnp.int32, (block, block), 0)
    limits = limit_ref[0]
    cosine, sine = cosine_ref[...], sine_ref[...]
    grad_rows_ref[...] = grad_ref[...].astype(jnp.float32).T
    mixed_rows_ref[...] = mixed_ref[...].astype(jnp.float32).T
    for kv in range(kv_width // HEAD_DIM):
        rows = slice(kv * HEAD_DIM, (kv + 1) * HEAD_DIM)
        value_rows = slice(kv_width + kv * HEAD_DIM, kv_width + (kv + 1) * HEAD_DIM)
        keys = [flipped(kv_ref[group, rows, :]) for group in range(groups)]
        values = [flipped(kv_ref[group, value_rows, :]) for group in range(groups)]
        for step in range(repeats):
            head = kv * repeats + step
            head_rows = slice(head * HEAD_DIM, (head + 1) * HEAD_DIM)
            query = query_ref[head_rows, :]
            query_tokens = flipped(query)
            grads = grad_rows_ref[head_rows, :]
            delta = jnp.sum(grads * mixed_rows_ref[head_rows, :], axis=0, keepdims=True)
            grads_low = grads.astype(jnp.bfloat16)
            grad_tokens = grads.T.astype(jnp.bfloat16)
            total = total_ref[0, head : head + 1, :]
            grad_query = None
            for group in range(groups):
                raw = jnp.dot(keys[group], query, preferred_element_type=jnp.float32)
                chances = jnp.where(
                    key_at < limits - group * block, jnp.exp2(raw * factor - total), 0.0
                )
                grad_chance = jnp.dot(
                    values[group], grads_low, preferred_element_type=jnp.float32
                )
                grad_score = (chances * (grad_chance - delta)).astype(jnp.bfloat16)
                part = jnp.dot(
                    kv_ref[group, rows, :], grad_score, preferred_element_type=jnp.float32
                )
                grad_query = part if grad_query is None else grad_query + part
                key_part = jnp.dot(
                    grad_score, query_tokens, preferred_element_type=jnp.float32
                )
                value_part = jnp.dot(
                    chances.astype(jnp.bfloat16), grad_tokens, preferred_element_type=jnp.float32
                )
                if step == 0:
                    key_sum_ref[group] = key_part
                    value_sum_ref[group] = value_part
                else:
                    key_sum_ref[group] += key_part
                    value_sum_ref[group] += value_part
            first, second = grad_query[:HALF] * scaling, grad_query[HALF:] * scaling
            query_rows_ref[head * HEAD_DIM : head * HEAD_DIM + HALF, :] = (
                first * cosine + second * sine
            )
            query_rows_ref[head * HEAD_DIM + HALF : (head + 1) * HEAD_DIM, :] = (
                second * cosine - first * sine
            )
        for group in range(groups):
            grad_kv_ref[group, rows, :] = (key_sum_ref[group].T * scaling).astype(jnp.bfloat16)
            grad_kv_ref[group, value_rows, :] = value_sum_ref[group].T.astype(jnp.bfloat16)
    grad_query_ref[...] = query_rows_ref[...].T.astype(jnp.bfloat16)


def attend_back(before, blocks, operands, repeats):
    query, kv_all, limits, _, _, grad_mixed, _, _ = operands
    query_width, tokens = query.shape
    groups, kv_rows, _ = kv_all.shape
    _, _, block = limits.shape
    heads = query_width // HEAD_DIM
    start, end = blocks
    pairs = query_width * (end - start) * block * groups * block
    by_column = pl.BlockSpec((query_width, block), lambda i: (0, i + start))
    by_row = pl.BlockSpec((block, query_width), lambda i: (i + start, 0))
    by_key = pl.BlockSpec((groups, kv_rows, block), lambda i: (0, 0, i + start))
    table = pl.BlockSpec((HALF, block), lambda i: (0, i + start))
    kept = () if before is None else tuple(before)

    def kernel(*refs):
        count = len(operands)
        attend_back_kernel(repeats, *refs[:count], *refs[count + len(kept) :])

    return pl.pallas_call(
        kernel,
        out_shape=(
            jax.ShapeDtypeStruct((tokens, query_width), jnp.bfloat16),
            jax.ShapeDtypeStruct(kv_all.shape, jnp.bfloat16),
        ),
        grid=(end - start,),
        in_specs=[
            by_column,
            by_key,
            pl.BlockSpec((1, 1, block), lambda i: (i + start, 0, 0)),
            pl.BlockSpec((1, heads, block), lambda i: (i + start, 0, 0)),
            by_row,
            pl.BlockSpec((block, query_width), lambda i: (i, 0)),
            table,
            table,
        ]
        + [pl.BlockSpec(memory_space=pl.ANY)] * len(kept),
        out_specs=(by_row, by_key),
        input_output_aliases={len(operands) + at: at for at in range(len(kept))},
        scratch_shapes=[
            pltpu.VMEM((query_width, block), jnp.float32),
            pltpu.VMEM((query_width, block), jnp.float32),
            pltpu.VMEM((query_width, block), jnp.float32),
            pltpu.VMEM((groups, block, HEAD_DIM), jnp.float32),
            pltpu.VMEM((groups, block, HEAD_DIM), jnp.float32),
        ],
        cost_estimate=pl.CostEstimate(
            flops=10 * pairs,
            bytes_accessed=2 * (end - start) * (4 * query.size + 2 * kv_all.size) // CHIPS,
            transcendentals=pairs // HEAD_DIM,
        ),
        name="attend_back",
    )(*operands, *kept)


def times(left, right):
    return jnp.dot(left, right, preferred_element_type=jnp.float32)


def times_t(left, right):
    return lax.dot_general(
        left, right, (((1,), (1,)), ((), ())), preferred_element_type=jnp.float32
    )


def inner_t(left, right):
    return lax.dot_general(
        left, right, (((0,), (0,)), ((), ())), preferred_element_type=jnp.float32
    )


def inverse_rms(values):
    return lax.rsqrt(jnp.mean(values * values, axis=-1, keepdims=True) + epsilon)


def norm_back(grad_normed, source, inverse, gain_full):
    weighted = grad_normed * gain_full
    average = jnp.mean(weighted * source, axis=-1, keepdims=True)
    return inverse * weighted - source * (inverse * inverse * inverse) * average


def limits_of(starts, places):
    limits = places + 1
    for which in range(2):
        inside = (places >= starts[which]) & (places < starts[which] + PIECE)
        limits = jnp.where(inside, starts[which] + PIECE, limits)
    return limits


def swap(value, flip):
    pairs = [(chip, chip ^ flip) for chip in range(CHIPS)]
    return lax.ppermute(value, "chip", pairs)


def collect(block):
    half = block.shape[0] // 2
    first = swap(block, 1)
    second = swap(block, 2)
    low = swap(first[:half], 2)
    high = swap(second[half:], 1)
    return [block, first, second, jnp.concatenate([low, high], axis=0)]


def give_back(left, right):
    return given(left, right, *to_give(left, right))


def to_give(left, right):
    low_type, wide_type = jnp.bfloat16, jnp.float32
    block = left.shape[0] // CHIPS
    half = block // 2
    third = times_t(left[3 * block :], right).astype(low_type)
    low = swap(third[:half], 1).astype(wide_type)
    high = swap(third[half:], 2).astype(wide_type)
    between = times_t(left[block : 3 * block], right).astype(low_type)
    first, second = between[:block], between[block:]
    for_first = jnp.concatenate(
        [first[:half], (first[half:].astype(wide_type) + high).astype(low_type)], axis=0
    )
    for_second = jnp.concatenate(
        [(second[:half].astype(wide_type) + low).astype(low_type), second[half:]], axis=0
    )
    return for_first, for_second


def given(left, right, for_first, for_second):
    block = left.shape[0] // CHIPS
    from_first = swap(for_first, 1).astype(jnp.float32)
    from_second = swap(for_second, 2).astype(jnp.float32)
    return times_t(left[:block], right) + from_first + from_second


def shards(
    layer_input,
    positions,
    piece_starts,
    gain_attn,
    w_query,
    w_key,
    w_value,
    w_out,
    gain_mlp,
    w_gate,
    w_up,
    w_down,
    out_grad,
):
    sequences, block_size, model_width = layer_input.shape
    assert sequences == 1
    groups = lax.axis_size("group")
    spread = lax.axis_size("dp")
    group_at, spread_at = lax.axis_index("group"), lax.axis_index("dp")
    chip, core = lax.axis_index("chip"), lax.axis_index("core")
    full_len = block_size * groups
    scaling = HEAD_DIM ** (-0.5)
    repeats = HEADS // KV_HEADS
    kv_own = KV_HEADS // CHIPS
    heads_own = HEADS // CHIPS
    query_width, kv_width = heads_own * HEAD_DIM, kv_own * HEAD_DIM
    half_rows = w_query.shape[0] // 2

    def own_part(weight):
        width = weight.shape[1] // CHIPS
        return lax.dynamic_slice(weight, (core * half_rows, chip * width), (half_rows, width))

    def gathered(*weights):
        part = jnp.concatenate([own_part(weight) for weight in weights], axis=1)
        return lax.all_gather(part, ("group", "core"), axis=0, tiled=True)

    gains = lax.all_gather(jnp.stack([gain_attn, gain_mlp]), "group", axis=1, tiled=True)
    gain_one, gain_two = gains[0].astype(jnp.float32), gains[1].astype(jnp.float32)

    w_attn = gathered(w_query, w_key, w_value, w_out)
    w_qkv, w_mix = w_attn[:, :-query_width], w_attn[:, -query_width:]
    w_lift = gathered(w_gate, w_up)
    w_sink = gathered(w_down)

    source_low = layer_input[0]
    source_all = jnp.concatenate(collect(source_low), axis=0).astype(jnp.float32)
    small = jnp.concatenate([positions[0], piece_starts[0]])
    smalls = jnp.stack([small, swap(small, 1), swap(small, 2), swap(small, 3)])
    places, starts_all = smalls[:, :block_size].reshape(-1), smalls[:, block_size:]
    grad_low = jnp.concatenate(collect(out_grad[0]), axis=0)

    normed_one = (source_all * inverse_rms(source_all) * gain_one).astype(jnp.bfloat16)
    cosine, sine = rope_tables(places)
    tokens = CHIPS * block_size
    lin = lax.dot_general(
        w_qkv, normed_one, (((0,), (1,)), ((), ())), preferred_element_type=jnp.float32
    )
    query_rot = rotate(lin[:query_width], cosine, sine).astype(jnp.bfloat16)
    key_rot = rotate(lin[query_width : query_width + kv_width], cosine, sine)
    kv_own_tokens = jnp.concatenate(
        [key_rot.astype(jnp.bfloat16), lin[query_width + kv_width :].astype(jnp.bfloat16)], axis=0
    )
    kv_all = lax.all_gather(kv_own_tokens, "group", axis=0, tiled=True)
    kv_all = kv_all.reshape(groups, 2 * kv_width, tokens)

    def reduced(total):
        return lax.psum_scatter(total, SUM_AXES, scatter_dimension=0, tiled=True)

    def product_low(left, right):
        return inner_t(left, right).astype(jnp.bfloat16)

    then = lax.optimization_barrier

    count = spread * CHIPS * 2
    whose = (spread_at * CHIPS + chip) * 2 + core

    def owned(total):
        rows, columns = total.shape[0] // CHIPS, total.shape[1]
        total = total.reshape(CHIPS, rows, columns)
        pieces = []
        for step in range(CHIPS):
            pairs = []
            for source_at in range(count):
                at_spread, at_chip, at_core = (
                    source_at // (2 * CHIPS),
                    source_at // 2 % CHIPS,
                    source_at % 2,
                )
                target = (at_core * spread + at_spread) * CHIPS + (at_chip ^ step)
                pairs.append((source_at, target))
            block = lax.dynamic_index_in_dim(total, chip ^ step, axis=0, keepdims=False)
            pieces.append(lax.ppermute(block, REPLICA, pairs))
        pieces = jnp.stack(pieces)
        return [
            lax.dynamic_index_in_dim(pieces, (whose % CHIPS) ^ at, axis=0, keepdims=False)
            for at in range(CHIPS)
        ]

    def laid(parts, start, width):
        parts = [part[:, start : start + width] for part in parts]
        return jnp.concatenate(parts, axis=1).astype(jnp.float32)

    query_places = group_at * block_size + jnp.arange(block_size, dtype=jnp.int32)
    limits = jnp.stack([limits_of(starts_all[which], query_places) for which in range(CHIPS)])
    limits = limits[:, None, :]
    mixed_low, log_totals = attend(query_rot, kv_all, limits, repeats)

    def from_group(values):
        return [
            lax.ppermute(
                lax.dynamic_index_in_dim(values, group_at ^ step, axis=0, keepdims=False),
                "group",
                [(at, at ^ step) for at in range(groups)],
            )
            for step in range(1, groups)
        ]

    source = source_low.astype(jnp.float32)
    inverse_one = inverse_rms(source)
    unit_one = source * inverse_one
    middle = source + give_back(mixed_low, w_mix)
    inverse_two = inverse_rms(middle)
    unit_two = middle * inverse_two
    normed_two = jnp.concatenate(collect((unit_two * gain_two).astype(jnp.bfloat16)), axis=0)
    wide = w_lift.shape[1] // 2
    both_up = times(normed_two, w_lift)
    gated, lifted = both_up[:, :wide], both_up[:, wide:]
    activated = jax.nn.silu(gated)
    hidden = (activated * lifted).astype(jnp.bfloat16)
    total_down, w_sink = then((product_low(grad_low, hidden), w_sink))
    sum_down = reduced(total_down)

    grad_hidden = times(grad_low, w_sink)
    sigmoid_gate = jax.nn.sigmoid(gated)
    grad_gate_low = (
        grad_hidden * lifted * (sigmoid_gate + gated * sigmoid_gate * (1.0 - sigmoid_gate))
    ).astype(jnp.bfloat16)
    grad_lift_low = (grad_hidden * activated).astype(jnp.bfloat16)
    grad_both = jnp.concatenate([grad_gate_low, grad_lift_low], axis=1)
    grad_normed_two = give_back(grad_both, w_lift)
    total_lift = product_low(normed_two, grad_both)
    grad_normed_two, sum_down, total_lift = then((grad_normed_two, sum_down, total_lift))
    sum_lift = reduced(total_lift)
    grad_middle = out_grad[0].astype(jnp.float32) + norm_back(
        grad_normed_two, middle, inverse_two, gain_two
    )
    grad_blocks = collect(grad_middle.astype(jnp.bfloat16))
    grads = None
    for blocks in ((0, 1), (1, 3), (3, 4)):
        if blocks[0] == 1:
            hidden, grads = then((hidden, grads))
            sink_out = to_give(hidden, w_sink)
        if blocks[0] == 3:
            sink_out, grad_blocks[3] = then((sink_out, grad_blocks[3]))
        grad_rows = jnp.concatenate(grad_blocks[slice(*blocks)], axis=0)
        grad_mixed_low = times(grad_rows, w_mix).astype(jnp.bfloat16)
        grads = attend_back(
            grads,
            blocks,
            (query_rot, kv_all, limits, log_totals, mixed_low, grad_mixed_low, cosine, sine),
            repeats,
        )
    grad_query_low, grad_kv = grads
    grad_middle_low = jnp.concatenate(grad_blocks, axis=0)
    output_full = middle + given(hidden, w_sink, *sink_out)
    grad_kv, sum_down = then((grad_kv, sum_down))
    squares = jnp.stack(
        [jnp.sum(source * source), jnp.sum(middle * middle), jnp.sum(output_full * output_full)]
    )
    place = core * spread + spread_at
    extra = jnp.where(jnp.arange(2 * spread)[:, None] == place, squares[None, :], 0.0)
    spare = -2 * kv_width % 128
    assert spare >= extra.size
    extra = jnp.pad(extra.reshape(1, -1), ((0, 0), (0, spare - extra.size)))
    extra = jnp.broadcast_to(extra, (model_width, spare)).astype(jnp.bfloat16)
    grad_kv_own = lax.dynamic_index_in_dim(grad_kv, group_at, axis=0, keepdims=False)
    grad_kv_others = from_group(grad_kv)
    attn_totals = with_layout_constraint(
        jnp.concatenate(
            [
                product_low(normed_one, grad_query_low),
                product_low(grad_middle_low, mixed_low),
                jnp.zeros((model_width, 2 * kv_width + spare), jnp.bfloat16),
            ],
            axis=1,
        ),
        Layout(major_to_minor=(0, 1)),
    )
    grad_down = laid(owned(sum_down), 0, wide)
    grad_kv_others[1], attn_totals, grad_down, extra = then(
        (grad_kv_others[1], attn_totals, grad_down, extra)
    )
    grad_kv = grad_kv_own.astype(jnp.float32)
    for part in grad_kv_others:
        grad_kv = grad_kv + part.astype(jnp.float32)
    grad_key = unrotate(grad_kv[:kv_width], cosine, sine)
    grad_kv_low = jnp.concatenate([grad_key, grad_kv[kv_width:]], axis=0).astype(jnp.bfloat16).T
    total_kv = jnp.concatenate([product_low(normed_one, grad_kv_low), extra], axis=1)
    attn_totals = lax.dynamic_update_slice(attn_totals, total_kv, (0, 2 * query_width))
    attn_totals, grad_query_low, sum_lift = then((attn_totals, grad_query_low, sum_lift))
    attn_sums = reduced(attn_totals)
    added = give_back(jnp.concatenate([grad_query_low, grad_kv_low], axis=1), w_qkv)
    input_grad = grad_middle + norm_back(added, source, inverse_one, gain_one)
    added, sum_lift = then((added, sum_lift))
    lift_parts = owned(sum_lift)
    grad_gate, grad_up = laid(lift_parts, 0, wide), laid(lift_parts, wide, wide)
    attn_parts = owned(attn_sums[:, :-spare])
    square_totals = lax.dynamic_slice(
        attn_sums[:1, -spare:].astype(jnp.float32), (0, place * 3), (1, 3)
    )
    stream_rms = jnp.sqrt(square_totals / (full_len * model_width))
    grad_query, grad_out = (laid(attn_parts, at * query_width, query_width) for at in range(2))
    grad_key, grad_value = (
        laid(attn_parts, 2 * query_width + at * kv_width, kv_width) for at in range(2)
    )

    def gain_grad(gain, *pairs):
        rows = pairs[0][1].shape[0]
        total = 0.0
        for weight, grad in pairs:
            weight = lax.dynamic_slice(weight, (whose * rows, 0), (rows, weight.shape[1]))
            total = total + jnp.sum(weight.astype(jnp.float32) * grad, axis=1)
        return total / lax.dynamic_slice(gain, (whose * rows,), (rows,)).astype(jnp.float32)

    grad_norm_mlp = gain_grad(gain_mlp, (w_gate, grad_gate), (w_up, grad_up))
    grad_norm_attn = gain_grad(
        gain_attn, (w_query, grad_query), (w_key, grad_key), (w_value, grad_value)
    )

    return (
        output_full.astype(jnp.bfloat16)[None],
        input_grad[None],
        grad_norm_attn,
        grad_query,
        grad_key,
        grad_value,
        grad_out,
        grad_norm_mlp,
        grad_gate,
        grad_up,
        grad_down,
        stream_rms,
    )


def solution(mesh):
    groups, replicas = mesh.shape["group"], mesh.shape["replica"]
    spread = replicas // (2 * CHIPS)
    devices = np.asarray(mesh.devices).reshape(groups, spread, CHIPS, 2)
    split = Mesh(devices, ("group", "dp", "chip", "core"))
    everyone = ("group",) + REPLICA
    placed = (
        P(REPLICA, "group", None),
        P(REPLICA, "group"),
        P(REPLICA, None),
        P("group"),
        P("group", None),
        P("group", None),
        P("group", None),
        P("group", None),
        P("group"),
        P("group", None),
        P("group", None),
        P("group", None),
        P(REPLICA, "group", None),
    )
    return jax.shard_map(
        shards,
        mesh=split,
        in_specs=placed,
        out_specs=(
            P(REPLICA, "group", None),
            P(REPLICA, "group", None),
            P(everyone),
            P(everyone, None),
            P(everyone, None),
            P(everyone, None),
            P(everyone, None),
            P(everyone),
            P(everyone, None),
            P(everyone, None),
            P(everyone, None),
            P(REPLICA, None),
        ),
        check_vma=False,
    )
```

```python
import numpy as np

import jax
import jax.numpy as jnp
from jax import lax
from jax.experimental import pallas as pl
from jax.experimental.pallas import tpu as pltpu
from jax.experimental.layout import Layout, with_layout_constraint
from jax.sharding import Mesh, PartitionSpec as P

HEADS = 32
KV_HEADS = 8
HEAD_DIM = 80
PIECE = 256

epsilon = 1e-05
rope_base = 1000000.0

CHIPS = 4
REPLICA = ("dp", "chip", "core")


HALF = HEAD_DIM // 2
LOG2E = 1.4426950408889634


def rope_tables(places):
    frequency = rope_base ** (-(jnp.arange(HALF, dtype=jnp.float32) * 2.0 / HEAD_DIM))
    angles = frequency[:, None] * places.astype(jnp.float32)[None, :]
    return (jnp.cos(angles), jnp.sin(angles))


def rotate(values, cosine, sine):
    first, second = halves_of(values)
    return joined(first * cosine - second * sine, second * cosine + first * sine)


def unrotate(grads, cosine, sine):
    first, second = halves_of(grads)
    return joined(first * cosine + second * sine, second * cosine - first * sine)


def halves_of(values):
    heads = values.reshape(-1, 2, HALF, values.shape[-1])
    return heads[:, 0], heads[:, 1]


def joined(first, second):
    return jnp.stack([first, second], axis=1).reshape(-1, first.shape[-1])


def flipped(values):
    return values.astype(jnp.float32).T.astype(jnp.bfloat16)


def attend_kernel(repeats, query_ref, kv_ref, limit_ref, mixed_ref, total_ref, out_ref):
    groups, kv_rows, block = kv_ref.shape
    kv_width = kv_rows // 2
    factor = HEAD_DIM ** (-0.5) * LOG2E
    key_at = lax.broadcasted_iota(jnp.int32, (block, block), 0)
    limits = limit_ref[0]
    for kv in range(kv_width // HEAD_DIM):
        rows = slice(kv * HEAD_DIM, (kv + 1) * HEAD_DIM)
        value_rows = slice(kv_width + kv * HEAD_DIM, kv_width + (kv + 1) * HEAD_DIM)
        keys = [flipped(kv_ref[group, rows, :]) for group in range(groups)]
        for head in range(kv * repeats, (kv + 1) * repeats):
            head_rows = slice(head * HEAD_DIM, (head + 1) * HEAD_DIM)
            query = query_ref[head_rows, :]
            scores = []
            for group in range(groups):
                raw = jnp.dot(keys[group], query, preferred_element_type=jnp.float32)
                scores.append(jnp.where(key_at < limits - group * block, raw, -1e30))
            highest = scores[0]
            for group in range(1, groups):
                highest = jnp.maximum(highest, scores[group])
            highest = jnp.max(highest, axis=0, keepdims=True) * factor
            row_sum, mixed = None, None
            for group in range(groups):
                raised = jnp.exp2(scores[group] * factor - highest)
                part_sum = jnp.sum(raised, axis=0, keepdims=True)
                part = jnp.dot(
                    kv_ref[group, value_rows, :],
                    raised.astype(jnp.bfloat16),
                    preferred_element_type=jnp.float32,
                )
                row_sum = part_sum if row_sum is None else row_sum + part_sum
                mixed = part if mixed is None else mixed + part
            out_ref[head_rows, :] = mixed / row_sum
            total_ref[0, head : head + 1, :] = highest + jnp.log2(row_sum)
    mixed_ref[...] = out_ref[...].T.astype(jnp.bfloat16)


def attend(query, kv_all, limits, repeats):
    query_width, tokens = query.shape
    groups, kv_rows, _ = kv_all.shape
    chips, _, block = limits.shape
    heads = query_width // HEAD_DIM
    pairs = query_width * tokens * groups * block
    return pl.pallas_call(
        lambda *refs: attend_kernel(repeats, *refs),
        out_shape=(
            jax.ShapeDtypeStruct((tokens, query_width), jnp.bfloat16),
            jax.ShapeDtypeStruct((chips, heads, block), jnp.float32),
        ),
        grid=(chips,),
        in_specs=[
            pl.BlockSpec((query_width, block), lambda i: (0, i)),
            pl.BlockSpec((groups, kv_rows, block), lambda i: (0, 0, i)),
            pl.BlockSpec((1, 1, block), lambda i: (i, 0, 0)),
        ],
        out_specs=(
            pl.BlockSpec((block, query_width), lambda i: (i, 0)),
            pl.BlockSpec((1, heads, block), lambda i: (i, 0, 0)),
        ),
        scratch_shapes=[pltpu.VMEM((query_width, block), jnp.float32)],
        cost_estimate=pl.CostEstimate(
            flops=4 * pairs,
            bytes_accessed=2 * (2 * query.size + kv_all.size),
            transcendentals=pairs // HEAD_DIM,
        ),
        name="attend",
    )(query, kv_all, limits)


def attend_back_kernel(
    repeats,
    query_ref,
    kv_ref,
    limit_ref,
    total_ref,
    mixed_ref,
    grad_ref,
    cosine_ref,
    sine_ref,
    grad_query_ref,
    grad_kv_ref,
    grad_rows_ref,
    mixed_rows_ref,
    query_rows_ref,
    key_sum_ref,
    value_sum_ref,
):
    groups, kv_rows, block = kv_ref.shape
    kv_width = kv_rows // 2
    scaling = HEAD_DIM ** (-0.5)
    factor = scaling * LOG2E
    key_at = lax.broadcasted_iota(jnp.int32, (block, block), 0)
    limits = limit_ref[0]
    cosine, sine = cosine_ref[...], sine_ref[...]
    grad_rows_ref[...] = grad_ref[...].astype(jnp.float32).T
    mixed_rows_ref[...] = mixed_ref[...].astype(jnp.float32).T
    for kv in range(kv_width // HEAD_DIM):
        rows = slice(kv * HEAD_DIM, (kv + 1) * HEAD_DIM)
        value_rows = slice(kv_width + kv * HEAD_DIM, kv_width + (kv + 1) * HEAD_DIM)
        keys = [flipped(kv_ref[group, rows, :]) for group in range(groups)]
        values = [flipped(kv_ref[group, value_rows, :]) for group in range(groups)]
        for step in range(repeats):
            head = kv * repeats + step
            head_rows = slice(head * HEAD_DIM, (head + 1) * HEAD_DIM)
            query = query_ref[head_rows, :]
            query_tokens = flipped(query)
            grads = grad_rows_ref[head_rows, :]
            delta = jnp.sum(grads * mixed_rows_ref[head_rows, :], axis=0, keepdims=True)
            grads_low = grads.astype(jnp.bfloat16)
            grad_tokens = grads.T.astype(jnp.bfloat16)
            total = total_ref[0, head : head + 1, :]
            grad_query = None
            for group in range(groups):
                raw = jnp.dot(keys[group], query, preferred_element_type=jnp.float32)
                chances = jnp.where(
                    key_at < limits - group * block, jnp.exp2(raw * factor - total), 0.0
                )
                grad_chance = jnp.dot(
                    values[group], grads_low, preferred_element_type=jnp.float32
                )
                grad_score = (chances * (grad_chance - delta)).astype(jnp.bfloat16)
                part = jnp.dot(
                    kv_ref[group, rows, :], grad_score, preferred_element_type=jnp.float32
                )
                grad_query = part if grad_query is None else grad_query + part
                key_part = jnp.dot(
                    grad_score, query_tokens, preferred_element_type=jnp.float32
                )
                value_part = jnp.dot(
                    chances.astype(jnp.bfloat16), grad_tokens, preferred_element_type=jnp.float32
                )
                if step == 0:
                    key_sum_ref[group] = key_part
                    value_sum_ref[group] = value_part
                else:
                    key_sum_ref[group] += key_part
                    value_sum_ref[group] += value_part
            first, second = grad_query[:HALF] * scaling, grad_query[HALF:] * scaling
            query_rows_ref[head * HEAD_DIM : head * HEAD_DIM + HALF, :] = (
                first * cosine + second * sine
            )
            query_rows_ref[head * HEAD_DIM + HALF : (head + 1) * HEAD_DIM, :] = (
                second * cosine - first * sine
            )
        for group in range(groups):
            grad_kv_ref[group, rows, :] = (key_sum_ref[group].T * scaling).astype(jnp.bfloat16)
            grad_kv_ref[group, value_rows, :] = value_sum_ref[group].T.astype(jnp.bfloat16)
    grad_query_ref[...] = query_rows_ref[...].T.astype(jnp.bfloat16)


def attend_back(before, blocks, operands, repeats):
    query, kv_all, limits, _, _, grad_mixed, _, _ = operands
    query_width, tokens = query.shape
    groups, kv_rows, _ = kv_all.shape
    _, _, block = limits.shape
    heads = query_width // HEAD_DIM
    start, end = blocks
    pairs = query_width * (end - start) * block * groups * block
    by_column = pl.BlockSpec((query_width, block), lambda i: (0, i + start))
    by_row = pl.BlockSpec((block, query_width), lambda i: (i + start, 0))
    by_key = pl.BlockSpec((groups, kv_rows, block), lambda i: (0, 0, i + start))
    table = pl.BlockSpec((HALF, block), lambda i: (0, i + start))
    kept = () if before is None else tuple(before)

    def kernel(*refs):
        count = len(operands)
        attend_back_kernel(repeats, *refs[:count], *refs[count + len(kept) :])

    return pl.pallas_call(
        kernel,
        out_shape=(
            jax.ShapeDtypeStruct((tokens, query_width), jnp.bfloat16),
            jax.ShapeDtypeStruct(kv_all.shape, jnp.bfloat16),
        ),
        grid=(end - start,),
        in_specs=[
            by_column,
            by_key,
            pl.BlockSpec((1, 1, block), lambda i: (i + start, 0, 0)),
            pl.BlockSpec((1, heads, block), lambda i: (i + start, 0, 0)),
            by_row,
            pl.BlockSpec((block, query_width), lambda i: (i, 0)),
            table,
            table,
        ]
        + [pl.BlockSpec(memory_space=pl.ANY)] * len(kept),
        out_specs=(by_row, by_key),
        input_output_aliases={len(operands) + at: at for at in range(len(kept))},
        scratch_shapes=[
            pltpu.VMEM((query_width, block), jnp.float32),
            pltpu.VMEM((query_width, block), jnp.float32),
            pltpu.VMEM((query_width, block), jnp.float32),
            pltpu.VMEM((groups, block, HEAD_DIM), jnp.float32),
            pltpu.VMEM((groups, block, HEAD_DIM), jnp.float32),
        ],
        cost_estimate=pl.CostEstimate(
            flops=10 * pairs,
            bytes_accessed=2 * (end - start) * (4 * query.size + 2 * kv_all.size) // CHIPS,
            transcendentals=pairs // HEAD_DIM,
        ),
        name="attend_back",
    )(*operands, *kept)


def times(left, right):
    return jnp.dot(left, right, preferred_element_type=jnp.float32)


def times_t(left, right):
    return lax.dot_general(
        left, right, (((1,), (1,)), ((), ())), preferred_element_type=jnp.float32
    )


def inner_t(left, right):
    return lax.dot_general(
        left, right, (((0,), (0,)), ((), ())), preferred_element_type=jnp.float32
    )


def inverse_rms(values):
    return lax.rsqrt(jnp.mean(values * values, axis=-1, keepdims=True) + epsilon)


def norm_back(grad_normed, source, inverse, gain_full):
    weighted = grad_normed * gain_full
    average = jnp.mean(weighted * source, axis=-1, keepdims=True)
    return inverse * weighted - source * (inverse * inverse * inverse) * average


def limits_of(starts, places):
    limits = places + 1
    for which in range(2):
        inside = (places >= starts[which]) & (places < starts[which] + PIECE)
        limits = jnp.where(inside, starts[which] + PIECE, limits)
    return limits


def swap(value, flip):
    pairs = [(chip, chip ^ flip) for chip in range(CHIPS)]
    return lax.ppermute(value, "chip", pairs)


def collect(block):
    half = block.shape[0] // 2
    first = swap(block, 1)
    second = swap(block, 2)
    low = swap(first[:half], 2)
    high = swap(second[half:], 1)
    return [block, first, second, jnp.concatenate([low, high], axis=0)]


def give_back(left, right):
    return given(left, right, *to_give(left, right))


def to_give(left, right):
    low_type, wide_type = jnp.bfloat16, jnp.float32
    block = left.shape[0] // CHIPS
    half = block // 2
    third = times_t(left[3 * block :], right).astype(low_type)
    low = swap(third[:half], 1).astype(wide_type)
    high = swap(third[half:], 2).astype(wide_type)
    between = times_t(left[block : 3 * block], right).astype(low_type)
    first, second = between[:block], between[block:]
    for_first = jnp.concatenate(
        [first[:half], (first[half:].astype(wide_type) + high).astype(low_type)], axis=0
    )
    for_second = jnp.concatenate(
        [(second[:half].astype(wide_type) + low).astype(low_type), second[half:]], axis=0
    )
    return for_first, for_second


def given(left, right, for_first, for_second):
    block = left.shape[0] // CHIPS
    from_first = swap(for_first, 1).astype(jnp.float32)
    from_second = swap(for_second, 2).astype(jnp.float32)
    return times_t(left[:block], right) + from_first + from_second


def shards(
    layer_input,
    positions,
    piece_starts,
    gain_attn,
    w_query,
    w_key,
    w_value,
    w_out,
    gain_mlp,
    w_gate,
    w_up,
    w_down,
    out_grad,
):
    sequences, block_size, model_width = layer_input.shape
    assert sequences == 1
    groups = lax.axis_size("group")
    spread = lax.axis_size("dp")
    group_at, spread_at = lax.axis_index("group"), lax.axis_index("dp")
    chip, core = lax.axis_index("chip"), lax.axis_index("core")
    full_len = block_size * groups
    scaling = HEAD_DIM ** (-0.5)
    repeats = HEADS // KV_HEADS
    kv_own = KV_HEADS // CHIPS
    heads_own = HEADS // CHIPS
    query_width, kv_width = heads_own * HEAD_DIM, kv_own * HEAD_DIM
    half_rows = w_query.shape[0] // 2

    def own_part(weight):
        width = weight.shape[1] // CHIPS
        return lax.dynamic_slice(weight, (core * half_rows, chip * width), (half_rows, width))

    def gathered(*weights):
        part = jnp.concatenate([own_part(weight) for weight in weights], axis=1)
        return lax.all_gather(part, ("group", "core"), axis=0, tiled=True)

    gains = lax.all_gather(jnp.stack([gain_attn, gain_mlp]), "group", axis=1, tiled=True)
    gain_one, gain_two = gains[0].astype(jnp.float32), gains[1].astype(jnp.float32)

    w_attn = gathered(w_query, w_key, w_value, w_out)
    w_qkv, w_mix = w_attn[:, :-query_width], w_attn[:, -query_width:]
    w_lift = gathered(w_gate, w_up)
    w_sink = gathered(w_down)

    source_low = layer_input[0]
    source_all = jnp.concatenate(collect(source_low), axis=0).astype(jnp.float32)
    small = jnp.concatenate([positions[0], piece_starts[0]])
    smalls = jnp.stack([small, swap(small, 1), swap(small, 2), swap(small, 3)])
    places, starts_all = smalls[:, :block_size].reshape(-1), smalls[:, block_size:]
    grad_low = jnp.concatenate(collect(out_grad[0]), axis=0)

    normed_one = (source_all * inverse_rms(source_all) * gain_one).astype(jnp.bfloat16)
    cosine, sine = rope_tables(places)
    tokens = CHIPS * block_size
    lin = lax.dot_general(
        w_qkv, normed_one, (((0,), (1,)), ((), ())), preferred_element_type=jnp.float32
    )
    query_rot = rotate(lin[:query_width], cosine, sine).astype(jnp.bfloat16)
    key_rot = rotate(lin[query_width : query_width + kv_width], cosine, sine)
    kv_own_tokens = jnp.concatenate(
        [key_rot.astype(jnp.bfloat16), lin[query_width + kv_width :].astype(jnp.bfloat16)], axis=0
    )
    kv_all = lax.all_gather(kv_own_tokens, "group", axis=0, tiled=True)
    kv_all = kv_all.reshape(groups, 2 * kv_width, tokens)

    def beside(value):
        return lax.ppermute(value, "core", [(0, 1), (1, 0)])

    def across(total):
        halves = total.reshape(groups, 2, half_rows, total.shape[1])
        own = lax.dynamic_index_in_dim(halves, core, axis=1, keepdims=False)
        out = lax.dynamic_index_in_dim(halves, 1 - core, axis=1, keepdims=False)
        back = beside(out)
        own = (own.astype(jnp.float32) + back.astype(jnp.float32)).astype(jnp.bfloat16)
        return own.reshape(groups * half_rows, total.shape[1])

    def reduced(total, axes=("group", "core", "dp")):
        return lax.psum_scatter(total, axes, scatter_dimension=0, tiled=True)

    def product_low(left, right):
        return inner_t(left, right).astype(jnp.bfloat16)

    then = lax.optimization_barrier

    count = spread * CHIPS * 2
    whose = (spread_at * CHIPS + chip) * 2 + core

    def owned(total):
        rows, columns = total.shape[0] // CHIPS, total.shape[1]
        total = total.reshape(CHIPS, rows, columns)
        pieces = []
        for step in range(CHIPS):
            pairs = []
            for source_at in range(count):
                at_spread, at_chip, at_core = (
                    source_at // (2 * CHIPS),
                    source_at // 2 % CHIPS,
                    source_at % 2,
                )
                target = (at_core * spread + at_spread) * CHIPS + (at_chip ^ step)
                pairs.append((source_at, target))
            block = lax.dynamic_index_in_dim(total, chip ^ step, axis=0, keepdims=False)
            pieces.append(lax.ppermute(block, REPLICA, pairs))
        pieces = jnp.stack(pieces)
        return [
            lax.dynamic_index_in_dim(pieces, (whose % CHIPS) ^ at, axis=0, keepdims=False)
            for at in range(CHIPS)
        ]

    def laid(parts, start, width):
        parts = [part[:, start : start + width] for part in parts]
        return jnp.concatenate(parts, axis=1).astype(jnp.float32)

    query_places = group_at * block_size + jnp.arange(block_size, dtype=jnp.int32)
    limits = jnp.stack([limits_of(starts_all[which], query_places) for which in range(CHIPS)])
    limits = limits[:, None, :]
    mixed_low, log_totals = attend(query_rot, kv_all, limits, repeats)

    def from_group(values):
        return [
            lax.ppermute(
                lax.dynamic_index_in_dim(values, group_at ^ step, axis=0, keepdims=False),
                "group",
                [(at, at ^ step) for at in range(groups)],
            )
            for step in range(1, groups)
        ]

    source = source_low.astype(jnp.float32)
    inverse_one = inverse_rms(source)
    unit_one = source * inverse_one
    middle = source + give_back(mixed_low, w_mix)
    inverse_two = inverse_rms(middle)
    unit_two = middle * inverse_two
    normed_two = jnp.concatenate(collect((unit_two * gain_two).astype(jnp.bfloat16)), axis=0)
    wide = w_lift.shape[1] // 2
    both_up = times(normed_two, w_lift)
    gated, lifted = both_up[:, :wide], both_up[:, wide:]
    activated = jax.nn.silu(gated)
    hidden = (activated * lifted).astype(jnp.bfloat16)
    normed_rows = normed_one.T.reshape(groups, 2, half_rows, tokens)
    own_rows = lax.dynamic_index_in_dim(normed_rows, core, axis=1, keepdims=False)
    other_rows = lax.dynamic_index_in_dim(normed_rows, 1 - core, axis=1, keepdims=False)
    pair_rows = jnp.concatenate([own_rows, beside(other_rows)], axis=2)
    pair_rows = pair_rows.reshape(groups * half_rows, 2 * tokens)
    hidden, pair_rows = then((hidden, pair_rows))
    total_down, w_sink = then((product_low(grad_low, hidden), w_sink))
    sum_down = reduced(total_down)

    grad_hidden = times(grad_low, w_sink)
    sigmoid_gate = jax.nn.sigmoid(gated)
    grad_gate_low = (
        grad_hidden * lifted * (sigmoid_gate + gated * sigmoid_gate * (1.0 - sigmoid_gate))
    ).astype(jnp.bfloat16)
    grad_lift_low = (grad_hidden * activated).astype(jnp.bfloat16)
    grad_both = jnp.concatenate([grad_gate_low, grad_lift_low], axis=1)
    grad_normed_two = give_back(grad_both, w_lift)
    total_lift = product_low(normed_two, grad_both)
    grad_normed_two, sum_down, total_lift = then((grad_normed_two, sum_down, total_lift))
    sum_lift = reduced(total_lift)
    grad_middle = out_grad[0].astype(jnp.float32) + norm_back(
        grad_normed_two, middle, inverse_two, gain_two
    )
    grad_blocks = collect(grad_middle.astype(jnp.bfloat16))
    grads = None
    for blocks in ((0, 1), (1, 3), (3, 4)):
        if blocks[0] == 1:
            hidden, grads = then((hidden, grads))
            sink_out = to_give(hidden, w_sink)
        if blocks[0] == 3:
            sink_out, grad_blocks[3] = then((sink_out, grad_blocks[3]))
        grad_rows = jnp.concatenate(grad_blocks[slice(*blocks)], axis=0)
        grad_mixed_low = times(grad_rows, w_mix).astype(jnp.bfloat16)
        grads = attend_back(
            grads,
            blocks,
            (query_rot, kv_all, limits, log_totals, mixed_low, grad_mixed_low, cosine, sine),
            repeats,
        )
    grad_query_low, grad_kv = grads
    grad_middle_low = jnp.concatenate(grad_blocks, axis=0)
    output_full = middle + given(hidden, w_sink, *sink_out)
    grad_kv, sum_down = then((grad_kv, sum_down))
    squares = jnp.stack(
        [jnp.sum(source * source), jnp.sum(middle * middle), jnp.sum(output_full * output_full)]
    )
    place = core * spread + spread_at
    extra = jnp.where(jnp.arange(2 * spread)[:, None] == place, squares[None, :], 0.0)
    spare = -2 * kv_width % 128
    assert spare >= extra.size
    extra = jnp.pad(extra.reshape(1, -1), ((0, 0), (0, spare - extra.size)))
    extra = jnp.broadcast_to(extra, (model_width // 2, spare)).astype(jnp.bfloat16)
    grad_kv_own = lax.dynamic_index_in_dim(grad_kv, group_at, axis=0, keepdims=False)
    grad_kv_others = from_group(grad_kv)
    attn_totals = with_layout_constraint(
        jnp.concatenate(
            [
                across(product_low(normed_one, grad_query_low)),
                across(product_low(grad_middle_low, mixed_low)),
                jnp.zeros((model_width // 2, 2 * kv_width + spare), jnp.bfloat16),
            ],
            axis=1,
        ),
        Layout(major_to_minor=(0, 1)),
    )
    grad_down = laid(owned(sum_down), 0, wide)
    grad_kv_others[1], attn_totals, grad_down, extra = then(
        (grad_kv_others[1], attn_totals, grad_down, extra)
    )
    grad_kv = grad_kv_own.astype(jnp.float32)
    for part in grad_kv_others:
        grad_kv = grad_kv + part.astype(jnp.float32)
    grad_key = unrotate(grad_kv[:kv_width], cosine, sine)
    grad_kv_rows = jnp.concatenate([grad_key, grad_kv[kv_width:]], axis=0).astype(jnp.bfloat16)
    grad_kv_low = grad_kv_rows.T
    pair_kv = jnp.concatenate([grad_kv_rows, beside(grad_kv_rows)], axis=1)
    total_kv = jnp.concatenate([times_t(pair_rows, pair_kv).astype(jnp.bfloat16), extra], axis=1)
    attn_totals = lax.dynamic_update_slice(attn_totals, total_kv, (0, 2 * query_width))
    attn_totals, grad_query_low, sum_lift = then((attn_totals, grad_query_low, sum_lift))
    attn_sums = reduced(attn_totals, ("group", "dp"))
    added = give_back(jnp.concatenate([grad_query_low, grad_kv_low], axis=1), w_qkv)
    input_grad = grad_middle + norm_back(added, source, inverse_one, gain_one)
    added, sum_lift = then((added, sum_lift))
    lift_parts = owned(sum_lift)
    grad_gate, grad_up = laid(lift_parts, 0, wide), laid(lift_parts, wide, wide)
    attn_parts = owned(attn_sums[:, :-spare])
    square_totals = lax.dynamic_slice(
        attn_sums[:1, -spare:].astype(jnp.float32), (0, place * 3), (1, 3)
    )
    stream_rms = jnp.sqrt(square_totals / (full_len * model_width))
    grad_query, grad_out = (laid(attn_parts, at * query_width, query_width) for at in range(2))
    grad_key, grad_value = (
        laid(attn_parts, 2 * query_width + at * kv_width, kv_width) for at in range(2)
    )

    def gain_grad(gain, parts, weights):
        rows = parts[0].shape[0]
        total = 0.0
        for at, part in enumerate(parts):
            columns = []
            for weight in weights:
                if isinstance(weight, int):
                    columns.append(jnp.zeros((rows, weight), jnp.bfloat16))
                else:
                    width = weight.shape[1] // CHIPS
                    start = (whose * rows, at * width)
                    columns.append(lax.dynamic_slice(weight, start, (rows, width)))
            columns = jnp.concatenate(columns, axis=1)
            total = total + columns.astype(jnp.float32) * part.astype(jnp.float32)
        total = jnp.sum(total, axis=1)
        return total / lax.dynamic_slice(gain, (whose * rows,), (rows,)).astype(jnp.float32)

    grad_norm_mlp = gain_grad(gain_mlp, lift_parts, (w_gate, w_up))
    grad_norm_attn = gain_grad(gain_attn, attn_parts, (w_query, query_width, w_key, w_value))

    return (
        output_full.astype(jnp.bfloat16)[None],
        input_grad[None],
        grad_norm_attn,
        grad_query,
        grad_key,
        grad_value,
        grad_out,
        grad_norm_mlp,
        grad_gate,
        grad_up,
        grad_down,
        stream_rms,
    )


def solution(mesh):
    groups, replicas = mesh.shape["group"], mesh.shape["replica"]
    spread = replicas // (2 * CHIPS)
    devices = np.asarray(mesh.devices).reshape(groups, spread, CHIPS, 2)
    split = Mesh(devices, ("group", "dp", "chip", "core"))
    everyone = ("group",) + REPLICA
    placed = (
        P(REPLICA, "group", None),
        P(REPLICA, "group"),
        P(REPLICA, None),
        P("group"),
        P("group", None),
        P("group", None),
        P("group", None),
        P("group", None),
        P("group"),
        P("group", None),
        P("group", None),
        P("group", None),
        P(REPLICA, "group", None),
    )
    return jax.shard_map(
        shards,
        mesh=split,
        in_specs=placed,
        out_specs=(
            P(REPLICA, "group", None),
            P(REPLICA, "group", None),
            P(everyone),
            P(everyone, None),
            P(everyone, None),
            P(everyone, None),
            P(everyone, None),
            P(everyone),
            P(everyone, None),
            P(everyone, None),
            P(everyone, None),
            P(REPLICA, None),
        ),
        check_vma=False,
    )
```

```python
import numpy as np

import jax
import jax.numpy as jnp
from jax import lax
from jax.experimental import pallas as pl
from jax.experimental.pallas import tpu as pltpu
from jax.experimental.layout import Layout, with_layout_constraint
from jax.sharding import Mesh, PartitionSpec as P

HEADS = 32
KV_HEADS = 8
HEAD_DIM = 80
PIECE = 256

epsilon = 1e-05
rope_base = 1000000.0

CHIPS = 4
REPLICA = ("dp", "chip", "core")


HALF = HEAD_DIM // 2
LOG2E = 1.4426950408889634


def rope_tables(places):
    frequency = rope_base ** (-(jnp.arange(HALF, dtype=jnp.float32) * 2.0 / HEAD_DIM))
    angles = frequency[:, None] * places.astype(jnp.float32)[None, :]
    return (jnp.cos(angles), jnp.sin(angles))


def rotate(values, cosine, sine):
    first, second = halves_of(values)
    return joined(first * cosine - second * sine, second * cosine + first * sine)


def unrotate(grads, cosine, sine):
    first, second = halves_of(grads)
    return joined(first * cosine + second * sine, second * cosine - first * sine)


def halves_of(values):
    heads = values.reshape(-1, 2, HALF, values.shape[-1])
    return heads[:, 0], heads[:, 1]


def joined(first, second):
    return jnp.stack([first, second], axis=1).reshape(-1, first.shape[-1])


def flipped(values):
    return values.astype(jnp.float32).T.astype(jnp.bfloat16)


def attend_kernel(repeats, query_ref, kv_ref, limit_ref, mixed_ref, total_ref, out_ref):
    groups, kv_rows, block = kv_ref.shape
    kv_width = kv_rows // 2
    factor = HEAD_DIM ** (-0.5) * LOG2E
    key_at = lax.broadcasted_iota(jnp.int32, (block, block), 0)
    limits = limit_ref[0]
    for kv in range(kv_width // HEAD_DIM):
        rows = slice(kv * HEAD_DIM, (kv + 1) * HEAD_DIM)
        value_rows = slice(kv_width + kv * HEAD_DIM, kv_width + (kv + 1) * HEAD_DIM)
        keys = [flipped(kv_ref[group, rows, :]) for group in range(groups)]
        for head in range(kv * repeats, (kv + 1) * repeats):
            head_rows = slice(head * HEAD_DIM, (head + 1) * HEAD_DIM)
            query = query_ref[head_rows, :]
            scores = []
            for group in range(groups):
                raw = jnp.dot(keys[group], query, preferred_element_type=jnp.float32)
                scores.append(jnp.where(key_at < limits - group * block, raw, -1e30))
            highest = scores[0]
            for group in range(1, groups):
                highest = jnp.maximum(highest, scores[group])
            highest = jnp.max(highest, axis=0, keepdims=True) * factor
            row_sum, mixed = None, None
            for group in range(groups):
                raised = jnp.exp2(scores[group] * factor - highest)
                part_sum = jnp.sum(raised, axis=0, keepdims=True)
                part = jnp.dot(
                    kv_ref[group, value_rows, :],
                    raised.astype(jnp.bfloat16),
                    preferred_element_type=jnp.float32,
                )
                row_sum = part_sum if row_sum is None else row_sum + part_sum
                mixed = part if mixed is None else mixed + part
            out_ref[head_rows, :] = mixed / row_sum
            total_ref[0, head : head + 1, :] = highest + jnp.log2(row_sum)
    mixed_ref[...] = out_ref[...].T.astype(jnp.bfloat16)


def attend(query, kv_all, limits, repeats):
    query_width, tokens = query.shape
    groups, kv_rows, _ = kv_all.shape
    chips, _, block = limits.shape
    heads = query_width // HEAD_DIM
    pairs = query_width * tokens * groups * block
    return pl.pallas_call(
        lambda *refs: attend_kernel(repeats, *refs),
        out_shape=(
            jax.ShapeDtypeStruct((tokens, query_width), jnp.bfloat16),
            jax.ShapeDtypeStruct((chips, heads, block), jnp.float32),
        ),
        grid=(chips,),
        in_specs=[
            pl.BlockSpec((query_width, block), lambda i: (0, i)),
            pl.BlockSpec((groups, kv_rows, block), lambda i: (0, 0, i)),
            pl.BlockSpec((1, 1, block), lambda i: (i, 0, 0)),
        ],
        out_specs=(
            pl.BlockSpec((block, query_width), lambda i: (i, 0)),
            pl.BlockSpec((1, heads, block), lambda i: (i, 0, 0)),
        ),
        scratch_shapes=[pltpu.VMEM((query_width, block), jnp.float32)],
        cost_estimate=pl.CostEstimate(
            flops=4 * pairs,
            bytes_accessed=2 * (2 * query.size + kv_all.size),
            transcendentals=pairs // HEAD_DIM,
        ),
        name="attend",
    )(query, kv_all, limits)


def attend_back_kernel(
    repeats,
    query_ref,
    kv_ref,
    limit_ref,
    total_ref,
    mixed_ref,
    grad_ref,
    cosine_ref,
    sine_ref,
    grad_query_ref,
    grad_kv_ref,
    grad_rows_ref,
    mixed_rows_ref,
    query_rows_ref,
    key_sum_ref,
    value_sum_ref,
):
    groups, kv_rows, block = kv_ref.shape
    kv_width = kv_rows // 2
    scaling = HEAD_DIM ** (-0.5)
    factor = scaling * LOG2E
    key_at = lax.broadcasted_iota(jnp.int32, (block, block), 0)
    limits = limit_ref[0]
    cosine, sine = cosine_ref[...], sine_ref[...]
    grad_rows_ref[...] = grad_ref[...].astype(jnp.float32).T
    mixed_rows_ref[...] = mixed_ref[...].astype(jnp.float32).T
    for kv in range(kv_width // HEAD_DIM):
        rows = slice(kv * HEAD_DIM, (kv + 1) * HEAD_DIM)
        value_rows = slice(kv_width + kv * HEAD_DIM, kv_width + (kv + 1) * HEAD_DIM)
        keys = [flipped(kv_ref[group, rows, :]) for group in range(groups)]
        values = [flipped(kv_ref[group, value_rows, :]) for group in range(groups)]
        for step in range(repeats):
            head = kv * repeats + step
            head_rows = slice(head * HEAD_DIM, (head + 1) * HEAD_DIM)
            query = query_ref[head_rows, :]
            query_tokens = flipped(query)
            grads = grad_rows_ref[head_rows, :]
            delta = jnp.sum(grads * mixed_rows_ref[head_rows, :], axis=0, keepdims=True)
            grads_low = grads.astype(jnp.bfloat16)
            grad_tokens = grads.T.astype(jnp.bfloat16)
            total = total_ref[0, head : head + 1, :]
            grad_query = None
            for group in range(groups):
                raw = jnp.dot(keys[group], query, preferred_element_type=jnp.float32)
                chances = jnp.where(
                    key_at < limits - group * block, jnp.exp2(raw * factor - total), 0.0
                )
                grad_chance = jnp.dot(
                    values[group], grads_low, preferred_element_type=jnp.float32
                )
                grad_score = (chances * (grad_chance - delta)).astype(jnp.bfloat16)
                part = jnp.dot(
                    kv_ref[group, rows, :], grad_score, preferred_element_type=jnp.float32
                )
                grad_query = part if grad_query is None else grad_query + part
                key_part = jnp.dot(
                    grad_score, query_tokens, preferred_element_type=jnp.float32
                )
                value_part = jnp.dot(
                    chances.astype(jnp.bfloat16), grad_tokens, preferred_element_type=jnp.float32
                )
                if step == 0:
                    key_sum_ref[group] = key_part
                    value_sum_ref[group] = value_part
                else:
                    key_sum_ref[group] += key_part
                    value_sum_ref[group] += value_part
            first, second = grad_query[:HALF] * scaling, grad_query[HALF:] * scaling
            query_rows_ref[head * HEAD_DIM : head * HEAD_DIM + HALF, :] = (
                first * cosine + second * sine
            )
            query_rows_ref[head * HEAD_DIM + HALF : (head + 1) * HEAD_DIM, :] = (
                second * cosine - first * sine
            )
        for group in range(groups):
            grad_kv_ref[group, rows, :] = (key_sum_ref[group].T * scaling).astype(jnp.bfloat16)
            grad_kv_ref[group, value_rows, :] = value_sum_ref[group].T.astype(jnp.bfloat16)
    grad_query_ref[...] = query_rows_ref[...].T.astype(jnp.bfloat16)


def attend_back(before, blocks, operands, repeats):
    query, kv_all, limits, _, _, grad_mixed, _, _ = operands
    query_width, tokens = query.shape
    groups, kv_rows, _ = kv_all.shape
    _, _, block = limits.shape
    heads = query_width // HEAD_DIM
    start, end = blocks
    pairs = query_width * (end - start) * block * groups * block
    by_column = pl.BlockSpec((query_width, block), lambda i: (0, i + start))
    by_row = pl.BlockSpec((block, query_width), lambda i: (i + start, 0))
    by_key = pl.BlockSpec((groups, kv_rows, block), lambda i: (0, 0, i + start))
    table = pl.BlockSpec((HALF, block), lambda i: (0, i + start))
    kept = () if before is None else tuple(before)

    def kernel(*refs):
        count = len(operands)
        attend_back_kernel(repeats, *refs[:count], *refs[count + len(kept) :])

    return pl.pallas_call(
        kernel,
        out_shape=(
            jax.ShapeDtypeStruct((tokens, query_width), jnp.bfloat16),
            jax.ShapeDtypeStruct(kv_all.shape, jnp.bfloat16),
        ),
        grid=(end - start,),
        in_specs=[
            by_column,
            by_key,
            pl.BlockSpec((1, 1, block), lambda i: (i + start, 0, 0)),
            pl.BlockSpec((1, heads, block), lambda i: (i + start, 0, 0)),
            by_row,
            pl.BlockSpec((block, query_width), lambda i: (i, 0)),
            table,
            table,
        ]
        + [pl.BlockSpec(memory_space=pl.ANY)] * len(kept),
        out_specs=(by_row, by_key),
        input_output_aliases={len(operands) + at: at for at in range(len(kept))},
        scratch_shapes=[
            pltpu.VMEM((query_width, block), jnp.float32),
            pltpu.VMEM((query_width, block), jnp.float32),
            pltpu.VMEM((query_width, block), jnp.float32),
            pltpu.VMEM((groups, block, HEAD_DIM), jnp.float32),
            pltpu.VMEM((groups, block, HEAD_DIM), jnp.float32),
        ],
        cost_estimate=pl.CostEstimate(
            flops=10 * pairs,
            bytes_accessed=2 * (end - start) * (4 * query.size + 2 * kv_all.size) // CHIPS,
            transcendentals=pairs // HEAD_DIM,
        ),
        name="attend_back",
    )(*operands, *kept)


def times(left, right):
    return jnp.dot(left, right, preferred_element_type=jnp.float32)


def times_t(left, right):
    return lax.dot_general(
        left, right, (((1,), (1,)), ((), ())), preferred_element_type=jnp.float32
    )


def inner_t(left, right):
    return lax.dot_general(
        left, right, (((0,), (0,)), ((), ())), preferred_element_type=jnp.float32
    )


def inverse_rms(values):
    return lax.rsqrt(jnp.mean(values * values, axis=-1, keepdims=True) + epsilon)


def norm_back(grad_normed, source, inverse, gain_full):
    weighted = grad_normed * gain_full
    average = jnp.mean(weighted * source, axis=-1, keepdims=True)
    return inverse * weighted - source * (inverse * inverse * inverse) * average


def limits_of(starts, places):
    limits = places + 1
    for which in range(2):
        inside = (places >= starts[which]) & (places < starts[which] + PIECE)
        limits = jnp.where(inside, starts[which] + PIECE, limits)
    return limits


def swap(value, flip):
    pairs = [(chip, chip ^ flip) for chip in range(CHIPS)]
    return lax.ppermute(value, "chip", pairs)


def collect(block):
    half = block.shape[0] // 2
    first = swap(block, 1)
    second = swap(block, 2)
    low = swap(first[:half], 2)
    high = swap(second[half:], 1)
    return [block, first, second, jnp.concatenate([low, high], axis=0)]


def give_back(left, right):
    return given(left, right, *to_give(left, right))


def to_give(left, right):
    low_type, wide_type = jnp.bfloat16, jnp.float32
    block = left.shape[0] // CHIPS
    half = block // 2
    third = times_t(left[3 * block :], right).astype(low_type)
    low = swap(third[:half], 1).astype(wide_type)
    high = swap(third[half:], 2).astype(wide_type)
    between = times_t(left[block : 3 * block], right).astype(low_type)
    first, second = between[:block], between[block:]
    for_first = jnp.concatenate(
        [first[:half], (first[half:].astype(wide_type) + high).astype(low_type)], axis=0
    )
    for_second = jnp.concatenate(
        [(second[:half].astype(wide_type) + low).astype(low_type), second[half:]], axis=0
    )
    return for_first, for_second


def given(left, right, for_first, for_second, after=()):
    block = left.shape[0] // CHIPS
    from_first, from_second = swap(for_first, 1), swap(for_second, 2)
    from_first, from_second, _ = lax.optimization_barrier((from_first, from_second, after))
    own = times_t(left[:block], right)
    return own + from_first.astype(jnp.float32) + from_second.astype(jnp.float32)


def shards(
    layer_input,
    positions,
    piece_starts,
    gain_attn,
    w_query,
    w_key,
    w_value,
    w_out,
    gain_mlp,
    w_gate,
    w_up,
    w_down,
    out_grad,
):
    sequences, block_size, model_width = layer_input.shape
    assert sequences == 1
    groups = lax.axis_size("group")
    spread = lax.axis_size("dp")
    group_at, spread_at = lax.axis_index("group"), lax.axis_index("dp")
    chip, core = lax.axis_index("chip"), lax.axis_index("core")
    full_len = block_size * groups
    scaling = HEAD_DIM ** (-0.5)
    repeats = HEADS // KV_HEADS
    kv_own = KV_HEADS // CHIPS
    heads_own = HEADS // CHIPS
    query_width, kv_width = heads_own * HEAD_DIM, kv_own * HEAD_DIM
    half_rows = w_query.shape[0] // 2

    def own_part(weight):
        width = weight.shape[1] // CHIPS
        return lax.dynamic_slice(weight, (core * half_rows, chip * width), (half_rows, width))

    def gathered(*weights):
        part = jnp.concatenate([own_part(weight) for weight in weights], axis=1)
        return lax.all_gather(part, ("group", "core"), axis=0, tiled=True)

    gains = lax.all_gather(jnp.stack([gain_attn, gain_mlp]), "group", axis=1, tiled=True)
    gain_one, gain_two = gains[0].astype(jnp.float32), gains[1].astype(jnp.float32)

    w_attn = gathered(w_query, w_key, w_value, w_out)
    w_qkv, w_mix = w_attn[:, :-query_width], w_attn[:, -query_width:]
    w_lift = gathered(w_gate, w_up)
    w_sink = gathered(w_down)

    source_low = layer_input[0]
    source_all = jnp.concatenate(collect(source_low), axis=0).astype(jnp.float32)
    small = jnp.concatenate([positions[0], piece_starts[0]])
    smalls = jnp.stack([small, swap(small, 1), swap(small, 2), swap(small, 3)])
    places, starts_all = smalls[:, :block_size].reshape(-1), smalls[:, block_size:]
    grad_low = jnp.concatenate(collect(out_grad[0]), axis=0)

    normed_one = (source_all * inverse_rms(source_all) * gain_one).astype(jnp.bfloat16)
    cosine, sine = rope_tables(places)
    tokens = CHIPS * block_size
    lin = lax.dot_general(
        w_qkv, normed_one, (((0,), (1,)), ((), ())), preferred_element_type=jnp.float32
    )
    query_rot = rotate(lin[:query_width], cosine, sine).astype(jnp.bfloat16)
    key_rot = rotate(lin[query_width : query_width + kv_width], cosine, sine)
    kv_own_tokens = jnp.concatenate(
        [key_rot.astype(jnp.bfloat16), lin[query_width + kv_width :].astype(jnp.bfloat16)], axis=0
    )
    kv_all = lax.all_gather(kv_own_tokens, "group", axis=0, tiled=True)
    kv_all = kv_all.reshape(groups, 2 * kv_width, tokens)

    def beside(value):
        return lax.ppermute(value, "core", [(0, 1), (1, 0)])

    def pair_of(normed):
        rows = normed.T.reshape(groups, 2, half_rows, tokens)
        own = lax.dynamic_index_in_dim(rows, core, axis=1, keepdims=False)
        out = lax.dynamic_index_in_dim(rows, 1 - core, axis=1, keepdims=False)
        pair = jnp.concatenate([own, beside(out)], axis=2)
        return pair.reshape(groups * half_rows, 2 * tokens)

    def across(total):
        halves = total.reshape(groups, 2, half_rows, total.shape[1])
        own = lax.dynamic_index_in_dim(halves, core, axis=1, keepdims=False)
        out = lax.dynamic_index_in_dim(halves, 1 - core, axis=1, keepdims=False)
        back = beside(out)
        own = (own.astype(jnp.float32) + back.astype(jnp.float32)).astype(jnp.bfloat16)
        return own.reshape(groups * half_rows, total.shape[1])

    def reduced(total, axes=("group", "core", "dp")):
        return lax.psum_scatter(total, axes, scatter_dimension=0, tiled=True)

    def product_low(left, right):
        return inner_t(left, right).astype(jnp.bfloat16)

    then = lax.optimization_barrier

    count = spread * CHIPS * 2
    whose = (spread_at * CHIPS + chip) * 2 + core

    def owned(total):
        rows, columns = total.shape[0] // CHIPS, total.shape[1]
        total = total.reshape(CHIPS, rows, columns)
        pieces = []
        for step in range(CHIPS):
            pairs = []
            for source_at in range(count):
                at_spread, at_chip, at_core = (
                    source_at // (2 * CHIPS),
                    source_at // 2 % CHIPS,
                    source_at % 2,
                )
                target = (at_core * spread + at_spread) * CHIPS + (at_chip ^ step)
                pairs.append((source_at, target))
            block = lax.dynamic_index_in_dim(total, chip ^ step, axis=0, keepdims=False)
            pieces.append(lax.ppermute(block, REPLICA, pairs))
        pieces = jnp.stack(pieces)
        return [
            lax.dynamic_index_in_dim(pieces, (whose % CHIPS) ^ at, axis=0, keepdims=False)
            for at in range(CHIPS)
        ]

    def laid(parts, start, width):
        parts = [part[:, start : start + width] for part in parts]
        return jnp.concatenate(parts, axis=1).astype(jnp.float32)

    query_places = group_at * block_size + jnp.arange(block_size, dtype=jnp.int32)
    limits = jnp.stack([limits_of(starts_all[which], query_places) for which in range(CHIPS)])
    limits = limits[:, None, :]
    mixed_low, log_totals = attend(query_rot, kv_all, limits, repeats)

    def from_group(values):
        return [
            lax.ppermute(
                lax.dynamic_index_in_dim(values, group_at ^ step, axis=0, keepdims=False),
                "group",
                [(at, at ^ step) for at in range(groups)],
            )
            for step in range(1, groups)
        ]

    source = source_low.astype(jnp.float32)
    inverse_one = inverse_rms(source)
    unit_one = source * inverse_one
    middle = source + give_back(mixed_low, w_mix)
    inverse_two = inverse_rms(middle)
    unit_two = middle * inverse_two
    normed_two = jnp.concatenate(collect((unit_two * gain_two).astype(jnp.bfloat16)), axis=0)
    wide = w_lift.shape[1] // 2
    both_up = times(normed_two, w_lift)
    gated, lifted = both_up[:, :wide], both_up[:, wide:]
    activated = jax.nn.silu(gated)
    hidden = (activated * lifted).astype(jnp.bfloat16)
    pair_rows, pair_rows_two = pair_of(normed_one), pair_of(normed_two)
    hidden, pair_rows, pair_rows_two = then((hidden, pair_rows, pair_rows_two))
    total_down, w_sink = then((product_low(grad_low, hidden), w_sink))
    sum_down = reduced(total_down)

    grad_hidden = times(grad_low, w_sink)
    sigmoid_gate = jax.nn.sigmoid(gated)
    grad_gate_low = (
        grad_hidden * lifted * (sigmoid_gate + gated * sigmoid_gate * (1.0 - sigmoid_gate))
    ).astype(jnp.bfloat16)
    grad_lift_low = (grad_hidden * activated).astype(jnp.bfloat16)
    grad_both = jnp.concatenate([grad_gate_low, grad_lift_low], axis=1)
    pair_both = jnp.concatenate([grad_both, beside(grad_both)], axis=0)
    total_lift = times(pair_rows_two, pair_both).astype(jnp.bfloat16)
    grad_normed_two = given(
        grad_both, w_lift, *to_give(grad_both, w_lift), (sum_down, total_lift)
    )
    sum_lift = reduced(total_lift, ("group", "dp"))
    grad_middle = out_grad[0].astype(jnp.float32) + norm_back(
        grad_normed_two, middle, inverse_two, gain_two
    )
    grad_blocks = collect(grad_middle.astype(jnp.bfloat16))
    grads = None
    for blocks in ((0, 1), (1, 3), (3, 4)):
        if blocks[0] == 1:
            hidden, grads = then((hidden, grads))
            sink_out = to_give(hidden, w_sink)
        if blocks[0] == 3:
            sink_out, grad_blocks[3] = then((sink_out, grad_blocks[3]))
        grad_rows = jnp.concatenate(grad_blocks[slice(*blocks)], axis=0)
        grad_mixed_low = times(grad_rows, w_mix).astype(jnp.bfloat16)
        grads = attend_back(
            grads,
            blocks,
            (query_rot, kv_all, limits, log_totals, mixed_low, grad_mixed_low, cosine, sine),
            repeats,
        )
    grad_query_low, grad_kv = grads
    grad_middle_low = jnp.concatenate(grad_blocks, axis=0)
    output_full = middle + given(hidden, w_sink, *sink_out)
    grad_kv, sum_down = then((grad_kv, sum_down))
    squares = jnp.stack(
        [jnp.sum(source * source), jnp.sum(middle * middle), jnp.sum(output_full * output_full)]
    )
    place = core * spread + spread_at
    extra = jnp.where(jnp.arange(2 * spread)[:, None] == place, squares[None, :], 0.0)
    spare = -2 * kv_width % 128
    assert spare >= extra.size
    extra = jnp.pad(extra.reshape(1, -1), ((0, 0), (0, spare - extra.size)))
    extra = jnp.broadcast_to(extra, (model_width // 2, spare)).astype(jnp.bfloat16)
    grad_kv_own = lax.dynamic_index_in_dim(grad_kv, group_at, axis=0, keepdims=False)
    grad_kv_others = from_group(grad_kv)
    attn_totals = with_layout_constraint(
        jnp.concatenate(
            [
                across(product_low(normed_one, grad_query_low)),
                across(product_low(grad_middle_low, mixed_low)),
                jnp.zeros((model_width // 2, 2 * kv_width + spare), jnp.bfloat16),
            ],
            axis=1,
        ),
        Layout(major_to_minor=(0, 1)),
    )
    grad_down = laid(owned(sum_down), 0, wide)
    grad_kv_others[1], attn_totals, grad_down, extra = then(
        (grad_kv_others[1], attn_totals, grad_down, extra)
    )
    grad_kv = grad_kv_own.astype(jnp.float32)
    for part in grad_kv_others:
        grad_kv = grad_kv + part.astype(jnp.float32)
    grad_key = unrotate(grad_kv[:kv_width], cosine, sine)
    grad_kv_rows = jnp.concatenate([grad_key, grad_kv[kv_width:]], axis=0).astype(jnp.bfloat16)
    grad_kv_low = grad_kv_rows.T
    pair_kv = jnp.concatenate([grad_kv_rows, beside(grad_kv_rows)], axis=1)
    total_kv = jnp.concatenate([times_t(pair_rows, pair_kv).astype(jnp.bfloat16), extra], axis=1)
    attn_totals = lax.dynamic_update_slice(attn_totals, total_kv, (0, 2 * query_width))
    attn_totals, grad_query_low, sum_lift = then((attn_totals, grad_query_low, sum_lift))
    attn_sums = reduced(attn_totals, ("group", "dp"))
    added = give_back(jnp.concatenate([grad_query_low, grad_kv_low], axis=1), w_qkv)
    input_grad = grad_middle + norm_back(added, source, inverse_one, gain_one)
    added, sum_lift = then((added, sum_lift))
    lift_parts = owned(sum_lift)
    grad_gate, grad_up = laid(lift_parts, 0, wide), laid(lift_parts, wide, wide)
    attn_parts = owned(attn_sums[:, :-spare])
    square_totals = lax.dynamic_slice(
        attn_sums[:1, -spare:].astype(jnp.float32), (0, place * 3), (1, 3)
    )
    stream_rms = jnp.sqrt(square_totals / (full_len * model_width))
    grad_query, grad_out = (laid(attn_parts, at * query_width, query_width) for at in range(2))
    grad_key, grad_value = (
        laid(attn_parts, 2 * query_width + at * kv_width, kv_width) for at in range(2)
    )

    def gain_grad(gain, parts, weights):
        rows = parts[0].shape[0]
        total = 0.0
        for at, part in enumerate(parts):
            columns = []
            for weight in weights:
                if isinstance(weight, int):
                    columns.append(jnp.zeros((rows, weight), jnp.bfloat16))
                else:
                    width = weight.shape[1] // CHIPS
                    start = (whose * rows, at * width)
                    columns.append(lax.dynamic_slice(weight, start, (rows, width)))
            columns = jnp.concatenate(columns, axis=1)
            total = total + columns.astype(jnp.float32) * part.astype(jnp.float32)
        total = jnp.sum(total, axis=1)
        return total / lax.dynamic_slice(gain, (whose * rows,), (rows,)).astype(jnp.float32)

    grad_norm_mlp = gain_grad(gain_mlp, lift_parts, (w_gate, w_up))
    grad_norm_attn = gain_grad(gain_attn, attn_parts, (w_query, query_width, w_key, w_value))

    return (
        output_full.astype(jnp.bfloat16)[None],
        input_grad[None],
        grad_norm_attn,
        grad_query,
        grad_key,
        grad_value,
        grad_out,
        grad_norm_mlp,
        grad_gate,
        grad_up,
        grad_down,
        stream_rms,
    )


def solution(mesh):
    groups, replicas = mesh.shape["group"], mesh.shape["replica"]
    spread = replicas // (2 * CHIPS)
    devices = np.asarray(mesh.devices).reshape(groups, spread, CHIPS, 2)
    split = Mesh(devices, ("group", "dp", "chip", "core"))
    everyone = ("group",) + REPLICA
    placed = (
        P(REPLICA, "group", None),
        P(REPLICA, "group"),
        P(REPLICA, None),
        P("group"),
        P("group", None),
        P("group", None),
        P("group", None),
        P("group", None),
        P("group"),
        P("group", None),
        P("group", None),
        P("group", None),
        P(REPLICA, "group", None),
    )
    return jax.shard_map(
        shards,
        mesh=split,
        in_specs=placed,
        out_specs=(
            P(REPLICA, "group", None),
            P(REPLICA, "group", None),
            P(everyone),
            P(everyone, None),
            P(everyone, None),
            P(everyone, None),
            P(everyone, None),
            P(everyone),
            P(everyone, None),
            P(everyone, None),
            P(everyone, None),
            P(REPLICA, None),
        ),
        check_vma=False,
    )
```

```python
import numpy as np

import jax
import jax.numpy as jnp
from jax import lax
from jax.experimental import pallas as pl
from jax.experimental.pallas import tpu as pltpu
from jax.experimental.layout import Layout, with_layout_constraint
from jax.sharding import Mesh, PartitionSpec as P

HEADS = 32
KV_HEADS = 8
HEAD_DIM = 80
PIECE = 256

epsilon = 1e-05
rope_base = 1000000.0

CHIPS = 4
REPLICA = ("dp", "chip", "core")


HALF = HEAD_DIM // 2
LOG2E = 1.4426950408889634


def rope_tables(places):
    frequency = rope_base ** (-(jnp.arange(HALF, dtype=jnp.float32) * 2.0 / HEAD_DIM))
    angles = frequency[:, None] * places.astype(jnp.float32)[None, :]
    return (jnp.cos(angles), jnp.sin(angles))


def rotate(values, cosine, sine):
    first, second = halves_of(values)
    return joined(first * cosine - second * sine, second * cosine + first * sine)


def unrotate(grads, cosine, sine):
    first, second = halves_of(grads)
    return joined(first * cosine + second * sine, second * cosine - first * sine)


def halves_of(values):
    heads = values.reshape(-1, 2, HALF, values.shape[-1])
    return heads[:, 0], heads[:, 1]


def joined(first, second):
    return jnp.stack([first, second], axis=1).reshape(-1, first.shape[-1])


def flipped(values):
    return values.astype(jnp.float32).T.astype(jnp.bfloat16)


def attend_kernel(repeats, query_ref, kv_ref, limit_ref, mixed_ref, total_ref, out_ref):
    groups, kv_rows, block = kv_ref.shape
    kv_width = kv_rows // 2
    factor = HEAD_DIM ** (-0.5) * LOG2E
    key_at = lax.broadcasted_iota(jnp.int32, (block, block), 0)
    limits = limit_ref[0]
    for kv in range(kv_width // HEAD_DIM):
        rows = slice(kv * HEAD_DIM, (kv + 1) * HEAD_DIM)
        value_rows = slice(kv_width + kv * HEAD_DIM, kv_width + (kv + 1) * HEAD_DIM)
        keys = [flipped(kv_ref[group, rows, :]) for group in range(groups)]
        for head in range(kv * repeats, (kv + 1) * repeats):
            head_rows = slice(head * HEAD_DIM, (head + 1) * HEAD_DIM)
            query = query_ref[head_rows, :]
            scores = []
            for group in range(groups):
                raw = jnp.dot(keys[group], query, preferred_element_type=jnp.float32)
                scores.append(jnp.where(key_at < limits - group * block, raw, -1e30))
            highest = scores[0]
            for group in range(1, groups):
                highest = jnp.maximum(highest, scores[group])
            highest = jnp.max(highest, axis=0, keepdims=True) * factor
            row_sum, mixed = None, None
            for group in range(groups):
                raised = jnp.exp2(scores[group] * factor - highest)
                part_sum = jnp.sum(raised, axis=0, keepdims=True)
                part = jnp.dot(
                    kv_ref[group, value_rows, :],
                    raised.astype(jnp.bfloat16),
                    preferred_element_type=jnp.float32,
                )
                row_sum = part_sum if row_sum is None else row_sum + part_sum
                mixed = part if mixed is None else mixed + part
            out_ref[head_rows, :] = mixed / row_sum
            total_ref[0, head : head + 1, :] = highest + jnp.log2(row_sum)
    mixed_ref[...] = out_ref[...].T.astype(jnp.bfloat16)


def attend(query, kv_all, limits, repeats):
    query_width, tokens = query.shape
    groups, kv_rows, _ = kv_all.shape
    chips, _, block = limits.shape
    heads = query_width // HEAD_DIM
    pairs = query_width * tokens * groups * block
    return pl.pallas_call(
        lambda *refs: attend_kernel(repeats, *refs),
        out_shape=(
            jax.ShapeDtypeStruct((tokens, query_width), jnp.bfloat16),
            jax.ShapeDtypeStruct((chips, heads, block), jnp.float32),
        ),
        grid=(chips,),
        in_specs=[
            pl.BlockSpec((query_width, block), lambda i: (0, i)),
            pl.BlockSpec((groups, kv_rows, block), lambda i: (0, 0, i)),
            pl.BlockSpec((1, 1, block), lambda i: (i, 0, 0)),
        ],
        out_specs=(
            pl.BlockSpec((block, query_width), lambda i: (i, 0)),
            pl.BlockSpec((1, heads, block), lambda i: (i, 0, 0)),
        ),
        scratch_shapes=[pltpu.VMEM((query_width, block), jnp.float32)],
        cost_estimate=pl.CostEstimate(
            flops=4 * pairs,
            bytes_accessed=2 * (2 * query.size + kv_all.size),
            transcendentals=pairs // HEAD_DIM,
        ),
        name="attend",
    )(query, kv_all, limits)


def attend_back_kernel(
    repeats,
    query_ref,
    kv_ref,
    limit_ref,
    total_ref,
    mixed_ref,
    grad_ref,
    cosine_ref,
    sine_ref,
    grad_query_ref,
    grad_kv_ref,
    grad_rows_ref,
    mixed_rows_ref,
    query_rows_ref,
    key_sum_ref,
    value_sum_ref,
):
    groups, kv_rows, block = kv_ref.shape
    kv_width = kv_rows // 2
    scaling = HEAD_DIM ** (-0.5)
    factor = scaling * LOG2E
    key_at = lax.broadcasted_iota(jnp.int32, (block, block), 0)
    limits = limit_ref[0]
    cosine, sine = cosine_ref[...], sine_ref[...]
    grad_rows_ref[...] = grad_ref[...].astype(jnp.float32).T
    mixed_rows_ref[...] = mixed_ref[...].astype(jnp.float32).T
    for kv in range(kv_width // HEAD_DIM):
        rows = slice(kv * HEAD_DIM, (kv + 1) * HEAD_DIM)
        value_rows = slice(kv_width + kv * HEAD_DIM, kv_width + (kv + 1) * HEAD_DIM)
        keys = [flipped(kv_ref[group, rows, :]) for group in range(groups)]
        values = [flipped(kv_ref[group, value_rows, :]) for group in range(groups)]
        for step in range(repeats):
            head = kv * repeats + step
            head_rows = slice(head * HEAD_DIM, (head + 1) * HEAD_DIM)
            query = query_ref[head_rows, :]
            query_tokens = flipped(query)
            grads = grad_rows_ref[head_rows, :]
            delta = jnp.sum(grads * mixed_rows_ref[head_rows, :], axis=0, keepdims=True)
            grads_low = grads.astype(jnp.bfloat16)
            grad_tokens = grads.T.astype(jnp.bfloat16)
            total = total_ref[0, head : head + 1, :]
            grad_query = None
            for group in range(groups):
                raw = jnp.dot(keys[group], query, preferred_element_type=jnp.float32)
                chances = jnp.where(
                    key_at < limits - group * block, jnp.exp2(raw * factor - total), 0.0
                )
                grad_chance = jnp.dot(
                    values[group], grads_low, preferred_element_type=jnp.float32
                )
                grad_score = (chances * (grad_chance - delta)).astype(jnp.bfloat16)
                part = jnp.dot(
                    kv_ref[group, rows, :], grad_score, preferred_element_type=jnp.float32
                )
                grad_query = part if grad_query is None else grad_query + part
                key_part = jnp.dot(
                    grad_score, query_tokens, preferred_element_type=jnp.float32
                )
                value_part = jnp.dot(
                    chances.astype(jnp.bfloat16), grad_tokens, preferred_element_type=jnp.float32
                )
                if step == 0:
                    key_sum_ref[group] = key_part
                    value_sum_ref[group] = value_part
                else:
                    key_sum_ref[group] += key_part
                    value_sum_ref[group] += value_part
            first, second = grad_query[:HALF] * scaling, grad_query[HALF:] * scaling
            query_rows_ref[head * HEAD_DIM : head * HEAD_DIM + HALF, :] = (
                first * cosine + second * sine
            )
            query_rows_ref[head * HEAD_DIM + HALF : (head + 1) * HEAD_DIM, :] = (
                second * cosine - first * sine
            )
        for group in range(groups):
            grad_kv_ref[group, rows, :] = (key_sum_ref[group].T * scaling).astype(jnp.bfloat16)
            grad_kv_ref[group, value_rows, :] = value_sum_ref[group].T.astype(jnp.bfloat16)
    grad_query_ref[...] = query_rows_ref[...].T.astype(jnp.bfloat16)


def attend_back(before, blocks, operands, repeats):
    query, kv_all, limits, _, _, grad_mixed, _, _ = operands
    query_width, tokens = query.shape
    groups, kv_rows, _ = kv_all.shape
    _, _, block = limits.shape
    heads = query_width // HEAD_DIM
    start, end = blocks
    pairs = query_width * (end - start) * block * groups * block
    by_column = pl.BlockSpec((query_width, block), lambda i: (0, i + start))
    by_row = pl.BlockSpec((block, query_width), lambda i: (i + start, 0))
    by_key = pl.BlockSpec((groups, kv_rows, block), lambda i: (0, 0, i + start))
    table = pl.BlockSpec((HALF, block), lambda i: (0, i + start))
    kept = () if before is None else tuple(before)

    def kernel(*refs):
        count = len(operands)
        attend_back_kernel(repeats, *refs[:count], *refs[count + len(kept) :])

    return pl.pallas_call(
        kernel,
        out_shape=(
            jax.ShapeDtypeStruct((tokens, query_width), jnp.bfloat16),
            jax.ShapeDtypeStruct(kv_all.shape, jnp.bfloat16),
        ),
        grid=(end - start,),
        in_specs=[
            by_column,
            by_key,
            pl.BlockSpec((1, 1, block), lambda i: (i + start, 0, 0)),
            pl.BlockSpec((1, heads, block), lambda i: (i + start, 0, 0)),
            by_row,
            pl.BlockSpec((block, query_width), lambda i: (i, 0)),
            table,
            table,
        ]
        + [pl.BlockSpec(memory_space=pl.ANY)] * len(kept),
        out_specs=(by_row, by_key),
        input_output_aliases={len(operands) + at: at for at in range(len(kept))},
        scratch_shapes=[
            pltpu.VMEM((query_width, block), jnp.float32),
            pltpu.VMEM((query_width, block), jnp.float32),
            pltpu.VMEM((query_width, block), jnp.float32),
            pltpu.VMEM((groups, block, HEAD_DIM), jnp.float32),
            pltpu.VMEM((groups, block, HEAD_DIM), jnp.float32),
        ],
        cost_estimate=pl.CostEstimate(
            flops=10 * pairs,
            bytes_accessed=2 * (end - start) * (4 * query.size + 2 * kv_all.size) // CHIPS,
            transcendentals=pairs // HEAD_DIM,
        ),
        name="attend_back",
    )(*operands, *kept)


def times(left, right):
    return jnp.dot(left, right, preferred_element_type=jnp.float32)


def times_t(left, right):
    return lax.dot_general(
        left, right, (((1,), (1,)), ((), ())), preferred_element_type=jnp.float32
    )


def inner_t(left, right):
    return lax.dot_general(
        left, right, (((0,), (0,)), ((), ())), preferred_element_type=jnp.float32
    )


def inverse_rms(values):
    return lax.rsqrt(jnp.mean(values * values, axis=-1, keepdims=True) + epsilon)


def norm_back(grad_normed, source, inverse, gain_full):
    weighted = grad_normed * gain_full
    average = jnp.mean(weighted * source, axis=-1, keepdims=True)
    return inverse * weighted - source * (inverse * inverse * inverse) * average


def limits_of(starts, places):
    limits = places + 1
    for which in range(2):
        inside = (places >= starts[which]) & (places < starts[which] + PIECE)
        limits = jnp.where(inside, starts[which] + PIECE, limits)
    return limits


def swap(value, flip):
    pairs = [(chip, chip ^ flip) for chip in range(CHIPS)]
    return lax.ppermute(value, "chip", pairs)


def collect(block):
    half = block.shape[0] // 2
    first = swap(block, 1)
    second = swap(block, 2)
    low = swap(first[:half], 2)
    high = swap(second[half:], 1)
    return [block, first, second, jnp.concatenate([low, high], axis=0)]


def give_back(left, right):
    return given(left, right, *to_give(left, right))


def to_give(left, right):
    low_type, wide_type = jnp.bfloat16, jnp.float32
    block = left.shape[0] // CHIPS
    half = block // 2
    third = times_t(left[3 * block :], right).astype(low_type)
    low = swap(third[:half], 1).astype(wide_type)
    high = swap(third[half:], 2).astype(wide_type)
    between = times_t(left[block : 3 * block], right).astype(low_type)
    first, second = between[:block], between[block:]
    for_first = jnp.concatenate(
        [first[:half], (first[half:].astype(wide_type) + high).astype(low_type)], axis=0
    )
    for_second = jnp.concatenate(
        [(second[:half].astype(wide_type) + low).astype(low_type), second[half:]], axis=0
    )
    return for_first, for_second


def given(left, right, for_first, for_second, after=()):
    block = left.shape[0] // CHIPS
    from_first, from_second = swap(for_first, 1), swap(for_second, 2)
    from_first, from_second, _ = lax.optimization_barrier((from_first, from_second, after))
    own = times_t(left[:block], right)
    return own + from_first.astype(jnp.float32) + from_second.astype(jnp.float32)


def shards(
    layer_input,
    positions,
    piece_starts,
    gain_attn,
    w_query,
    w_key,
    w_value,
    w_out,
    gain_mlp,
    w_gate,
    w_up,
    w_down,
    out_grad,
):
    sequences, block_size, model_width = layer_input.shape
    assert sequences == 1
    groups = lax.axis_size("group")
    spread = lax.axis_size("dp")
    group_at, spread_at = lax.axis_index("group"), lax.axis_index("dp")
    chip, core = lax.axis_index("chip"), lax.axis_index("core")
    full_len = block_size * groups
    scaling = HEAD_DIM ** (-0.5)
    repeats = HEADS // KV_HEADS
    kv_own = KV_HEADS // CHIPS
    heads_own = HEADS // CHIPS
    query_width, kv_width = heads_own * HEAD_DIM, kv_own * HEAD_DIM
    half_rows = w_query.shape[0] // 2

    def own_part(weight):
        width = weight.shape[1] // CHIPS
        return lax.dynamic_slice(weight, (core * half_rows, chip * width), (half_rows, width))

    def gathered(*weights):
        part = jnp.concatenate([own_part(weight) for weight in weights], axis=1)
        return lax.all_gather(part, ("group", "core"), axis=0, tiled=True)

    gains = lax.all_gather(jnp.stack([gain_attn, gain_mlp]), "group", axis=1, tiled=True)
    gain_one, gain_two = gains[0].astype(jnp.float32), gains[1].astype(jnp.float32)

    w_attn = gathered(w_query, w_key, w_value, w_out)
    w_qkv, w_mix = w_attn[:, :-query_width], w_attn[:, -query_width:]
    w_lift = gathered(w_gate, w_up)
    w_sink = gathered(w_down)

    source_low = layer_input[0]
    source_all = jnp.concatenate(collect(source_low), axis=0).astype(jnp.float32)
    small = jnp.concatenate([positions[0], piece_starts[0]])
    smalls = jnp.stack([small, swap(small, 1), swap(small, 2), swap(small, 3)])
    places, starts_all = smalls[:, :block_size].reshape(-1), smalls[:, block_size:]
    grad_low = jnp.concatenate(collect(out_grad[0]), axis=0)

    normed_one = (source_all * inverse_rms(source_all) * gain_one).astype(jnp.bfloat16)
    cosine, sine = rope_tables(places)
    tokens = CHIPS * block_size
    lin = lax.dot_general(
        w_qkv, normed_one, (((0,), (1,)), ((), ())), preferred_element_type=jnp.float32
    )
    query_rot = rotate(lin[:query_width], cosine, sine).astype(jnp.bfloat16)
    key_rot = rotate(lin[query_width : query_width + kv_width], cosine, sine)
    kv_own_tokens = jnp.concatenate(
        [key_rot.astype(jnp.bfloat16), lin[query_width + kv_width :].astype(jnp.bfloat16)], axis=0
    )
    kv_all = lax.all_gather(kv_own_tokens, "group", axis=0, tiled=True)
    kv_all = kv_all.reshape(groups, 2 * kv_width, tokens)

    def beside(value):
        return lax.ppermute(value, "core", [(0, 1), (1, 0)])

    def pair_of(normed):
        rows = normed.T.reshape(groups, 2, half_rows, tokens)
        own = lax.dynamic_index_in_dim(rows, core, axis=1, keepdims=False)
        out = lax.dynamic_index_in_dim(rows, 1 - core, axis=1, keepdims=False)
        pair = jnp.concatenate([own, beside(out)], axis=2)
        return pair.reshape(groups * half_rows, 2 * tokens)

    def across(total):
        halves = total.reshape(groups, 2, half_rows, total.shape[1])
        own = lax.dynamic_index_in_dim(halves, core, axis=1, keepdims=False)
        out = lax.dynamic_index_in_dim(halves, 1 - core, axis=1, keepdims=False)
        back = beside(out)
        own = (own.astype(jnp.float32) + back.astype(jnp.float32)).astype(jnp.bfloat16)
        return own.reshape(groups * half_rows, total.shape[1])

    def reduced(total, axes=("group", "core", "dp")):
        return lax.psum_scatter(total, axes, scatter_dimension=0, tiled=True)

    def product_low(left, right):
        return inner_t(left, right).astype(jnp.bfloat16)

    then = lax.optimization_barrier

    count = spread * CHIPS * 2
    whose = (spread_at * CHIPS + chip) * 2 + core

    def owned(total):
        rows, columns = total.shape[0] // CHIPS, total.shape[1]
        total = total.reshape(CHIPS, rows, columns)
        pieces = []
        for step in range(CHIPS):
            pairs = []
            for source_at in range(count):
                at_spread, at_chip, at_core = (
                    source_at // (2 * CHIPS),
                    source_at // 2 % CHIPS,
                    source_at % 2,
                )
                target = (at_core * spread + at_spread) * CHIPS + (at_chip ^ step)
                pairs.append((source_at, target))
            block = lax.dynamic_index_in_dim(total, chip ^ step, axis=0, keepdims=False)
            pieces.append(lax.ppermute(block, REPLICA, pairs))
        pieces = jnp.stack(pieces)
        return [
            lax.dynamic_index_in_dim(pieces, (whose % CHIPS) ^ at, axis=0, keepdims=False)
            for at in range(CHIPS)
        ]

    def laid(parts, start, width):
        parts = [part[:, start : start + width] for part in parts]
        return jnp.concatenate(parts, axis=1).astype(jnp.float32)

    query_places = group_at * block_size + jnp.arange(block_size, dtype=jnp.int32)
    limits = jnp.stack([limits_of(starts_all[which], query_places) for which in range(CHIPS)])
    limits = limits[:, None, :]
    mixed_low, log_totals = attend(query_rot, kv_all, limits, repeats)

    def from_group(values):
        return [
            lax.ppermute(
                lax.dynamic_index_in_dim(values, group_at ^ step, axis=0, keepdims=False),
                "group",
                [(at, at ^ step) for at in range(groups)],
            )
            for step in range(1, groups)
        ]

    source = source_low.astype(jnp.float32)
    inverse_one = inverse_rms(source)
    unit_one = source * inverse_one
    middle = source + give_back(mixed_low, w_mix)
    inverse_two = inverse_rms(middle)
    unit_two = middle * inverse_two
    normed_two = jnp.concatenate(collect((unit_two * gain_two).astype(jnp.bfloat16)), axis=0)
    wide = w_lift.shape[1] // 2
    both_up = times(normed_two, w_lift)
    gated, lifted = both_up[:, :wide], both_up[:, wide:]
    activated = jax.nn.silu(gated)
    hidden = (activated * lifted).astype(jnp.bfloat16)
    pair_rows, pair_rows_two = pair_of(normed_one), pair_of(normed_two)
    hidden, pair_rows, pair_rows_two = then((hidden, pair_rows, pair_rows_two))
    total_down, w_sink = then((product_low(grad_low, hidden), w_sink))
    sum_down = reduced(total_down)

    grad_hidden = times(grad_low, w_sink)
    sigmoid_gate = jax.nn.sigmoid(gated)
    grad_gate_low = (
        grad_hidden * lifted * (sigmoid_gate + gated * sigmoid_gate * (1.0 - sigmoid_gate))
    ).astype(jnp.bfloat16)
    grad_lift_low = (grad_hidden * activated).astype(jnp.bfloat16)
    grad_both = jnp.concatenate([grad_gate_low, grad_lift_low], axis=1)
    pair_both = jnp.concatenate([grad_both, beside(grad_both)], axis=0)
    total_lift = times(pair_rows_two, pair_both).astype(jnp.bfloat16)
    grad_normed_two = given(
        grad_both, w_lift, *to_give(grad_both, w_lift), (sum_down, total_lift)
    )
    sum_lift = reduced(total_lift, ("group", "dp"))
    grad_middle = out_grad[0].astype(jnp.float32) + norm_back(
        grad_normed_two, middle, inverse_two, gain_two
    )
    grad_blocks = collect(grad_middle.astype(jnp.bfloat16))
    grads = None
    for blocks in ((0, 1), (1, 3), (3, 4)):
        if blocks[0] == 1:
            hidden, grads = then((hidden, grads))
            sink_out = to_give(hidden, w_sink)
        if blocks[0] == 3:
            sink_out, grad_blocks[3] = then((sink_out, grad_blocks[3]))
        grad_rows = jnp.concatenate(grad_blocks[slice(*blocks)], axis=0)
        grad_mixed_low = times(grad_rows, w_mix).astype(jnp.bfloat16)
        grads = attend_back(
            grads,
            blocks,
            (query_rot, kv_all, limits, log_totals, mixed_low, grad_mixed_low, cosine, sine),
            repeats,
        )
    grad_query_low, grad_kv = grads
    grad_middle_low = jnp.concatenate(grad_blocks, axis=0)
    grad_kv_own = lax.dynamic_index_in_dim(grad_kv, group_at, axis=0, keepdims=False)
    grad_kv_others = from_group(grad_kv)
    grad_kv_others[0], grad_query_low, grad_middle_low, sum_down, sink_out = then(
        (grad_kv_others[0], grad_query_low, grad_middle_low, sum_down, sink_out)
    )
    output_full = middle + given(hidden, w_sink, *sink_out)
    squares = jnp.stack(
        [jnp.sum(source * source), jnp.sum(middle * middle), jnp.sum(output_full * output_full)]
    )
    place = core * spread + spread_at
    extra = jnp.where(jnp.arange(2 * spread)[:, None] == place, squares[None, :], 0.0)
    spare = -2 * kv_width % 128
    assert spare >= extra.size
    extra = jnp.pad(extra.reshape(1, -1), ((0, 0), (0, spare - extra.size)))
    extra = jnp.broadcast_to(extra, (model_width // 2, spare)).astype(jnp.bfloat16)
    attn_totals = with_layout_constraint(
        jnp.concatenate(
            [
                across(product_low(normed_one, grad_query_low)),
                across(product_low(grad_middle_low, mixed_low)),
                jnp.zeros((model_width // 2, 2 * kv_width + spare), jnp.bfloat16),
            ],
            axis=1,
        ),
        Layout(major_to_minor=(0, 1)),
    )
    grad_down = laid(owned(sum_down), 0, wide)
    grad_kv_others[1], attn_totals, grad_down, extra = then(
        (grad_kv_others[1], attn_totals, grad_down, extra)
    )
    grad_kv = grad_kv_own.astype(jnp.float32)
    for part in grad_kv_others:
        grad_kv = grad_kv + part.astype(jnp.float32)
    grad_key = unrotate(grad_kv[:kv_width], cosine, sine)
    grad_kv_rows = jnp.concatenate([grad_key, grad_kv[kv_width:]], axis=0).astype(jnp.bfloat16)
    grad_kv_low = grad_kv_rows.T
    pair_kv = jnp.concatenate([grad_kv_rows, beside(grad_kv_rows)], axis=1)
    total_kv = jnp.concatenate([times_t(pair_rows, pair_kv).astype(jnp.bfloat16), extra], axis=1)
    attn_totals = lax.dynamic_update_slice(attn_totals, total_kv, (0, 2 * query_width))
    attn_totals, grad_query_low, sum_lift = then((attn_totals, grad_query_low, sum_lift))
    attn_sums = reduced(attn_totals, ("group", "dp"))
    added = give_back(jnp.concatenate([grad_query_low, grad_kv_low], axis=1), w_qkv)
    input_grad = grad_middle + norm_back(added, source, inverse_one, gain_one)
    added, sum_lift = then((added, sum_lift))
    lift_parts = owned(sum_lift)
    grad_gate, grad_up = laid(lift_parts, 0, wide), laid(lift_parts, wide, wide)
    attn_parts = owned(attn_sums[:, :-spare])
    square_totals = lax.dynamic_slice(
        attn_sums[:1, -spare:].astype(jnp.float32), (0, place * 3), (1, 3)
    )
    stream_rms = jnp.sqrt(square_totals / (full_len * model_width))
    grad_query, grad_out = (laid(attn_parts, at * query_width, query_width) for at in range(2))
    grad_key, grad_value = (
        laid(attn_parts, 2 * query_width + at * kv_width, kv_width) for at in range(2)
    )

    def gain_grad(gain, parts, weights):
        rows = parts[0].shape[0]
        total = 0.0
        for at, part in enumerate(parts):
            columns = []
            for weight in weights:
                if isinstance(weight, int):
                    columns.append(jnp.zeros((rows, weight), jnp.bfloat16))
                else:
                    width = weight.shape[1] // CHIPS
                    start = (whose * rows, at * width)
                    columns.append(lax.dynamic_slice(weight, start, (rows, width)))
            columns = jnp.concatenate(columns, axis=1)
            total = total + columns.astype(jnp.float32) * part.astype(jnp.float32)
        total = jnp.sum(total, axis=1)
        return total / lax.dynamic_slice(gain, (whose * rows,), (rows,)).astype(jnp.float32)

    grad_norm_mlp = gain_grad(gain_mlp, lift_parts, (w_gate, w_up))
    grad_norm_attn = gain_grad(gain_attn, attn_parts, (w_query, query_width, w_key, w_value))

    return (
        output_full.astype(jnp.bfloat16)[None],
        input_grad[None],
        grad_norm_attn,
        grad_query,
        grad_key,
        grad_value,
        grad_out,
        grad_norm_mlp,
        grad_gate,
        grad_up,
        grad_down,
        stream_rms,
    )


def solution(mesh):
    groups, replicas = mesh.shape["group"], mesh.shape["replica"]
    spread = replicas // (2 * CHIPS)
    devices = np.asarray(mesh.devices).reshape(groups, spread, CHIPS, 2)
    split = Mesh(devices, ("group", "dp", "chip", "core"))
    everyone = ("group",) + REPLICA
    placed = (
        P(REPLICA, "group", None),
        P(REPLICA, "group"),
        P(REPLICA, None),
        P("group"),
        P("group", None),
        P("group", None),
        P("group", None),
        P("group", None),
        P("group"),
        P("group", None),
        P("group", None),
        P("group", None),
        P(REPLICA, "group", None),
    )
    return jax.shard_map(
        shards,
        mesh=split,
        in_specs=placed,
        out_specs=(
            P(REPLICA, "group", None),
            P(REPLICA, "group", None),
            P(everyone),
            P(everyone, None),
            P(everyone, None),
            P(everyone, None),
            P(everyone, None),
            P(everyone),
            P(everyone, None),
            P(everyone, None),
            P(everyone, None),
            P(REPLICA, None),
        ),
        check_vma=False,
    )
```
